256 devices in a mesh: req: 32 (over z_hi, y, x), tp: 8 (over z_lo, core).
Axes of the slice: x: 4, y: 4, z: 8 (z_hi: 2, z_lo: 4; z = z_hi * 4 + z_lo), core: 2. Of those that a mesh axis runs over, the one named last changes fastest.
Arguments:
- queries: bfloat16 [64, 256, 16, 256], P('req', None, 'tp'), may hold values from -6 to 6
- suffix_kv: bfloat16 [64, 256, 8, 512], P('req', None, 'tp'), may hold values from -6 to 6
- prefix_kv: bfloat16 [32, 1024, 8, 512], P('req', None, 'tp'), may hold values from -6 to 6
- out_weight: bfloat16 [4096, 3584], P('tp'), may hold values from -0.09375 to 0.09375
- residual: bfloat16 [64, 256, 3584], P('req', None, 'tp'), may hold values from -6 to 6
- norm_gain: float32 [3584], P('tp'), may hold values from 0.5 to 1.5
- suffix_len: int32 [64], replicated, may hold values from 1 to 256, 8192 in all
- member: int32 [64], replicated, may hold values from 0 to 63, each once
- owner: int32 [8], replicated, may hold values from 0 to 31, as said below
- assign: int32 [64], replicated, may hold values from 0 to 63, each once
Outputs:
- block_out: bfloat16 [64, 256, 3584], P('req', None, 'tp')
The draws below stay inside these ranges and needn't reach their ends.
Inputs may be any that keep to these rules, and one draw needn't show every extreme that they name: `owner`: distinct req indices.
All inputs are finite; a program needn't handle non-finite values.
Results may differ from the reference program's by a relative error of at most 0.011.
Values may be sent and summed in bfloat16 or wider, within the bound.
A program may use at most 64 MiB of HBM per device.

```python
import math
import jax
import jax.numpy as jnp
import numpy as np
from jax import lax

D = 3584
HEADS = 16
KVH = 8
HD = 256
SUF_MAX = 256
PREFIX = 1024
GROUPS = 8
REQUESTS = 64
N_REQ = 32
N_TP = 8


def draw_owner(key, part):
    first_key = jax.random.fold_in(key, 11)
    second_key = jax.random.fold_in(key, 23)
    inner = jax.random.permutation(first_key, N_REQ - 2)[:GROUPS - 2] + 1
    full = jnp.concatenate([jnp.zeros((1,), jnp.int32), inner.astype(jnp.int32), jnp.full((1,), N_REQ - 1, jnp.int32)])
    return jax.random.permutation(second_key, full).astype(jnp.int32)


def levels(stream_key, dims, shards, low, largest):
    level, own = 1.0, jax.random.fold_in(stream_key, 6)
    for position, parts in shards:
        draws = jnp.exp(jax.random.uniform(jax.random.fold_in(own, position), (parts,), jnp.float32, low / len(shards), largest / len(shards)))
        level = level * jnp.repeat(draws, dims[position] // parts).reshape([-1 if axis == position else 1 for axis in range(len(dims))])
    return level


def length_profile(count, total, reach, skew):
    weights = [(1 << 20) // math.isqrt(rank ** skew) + 1 for rank in range(2, count + 1)]
    spare, counts = total - reach - (count - 1), [1] * (count - 1)
    while spare > 0:
        free = [i for i in range(count - 1) if counts[i] < reach]
        pool, remaining = sum([weights[i] for i in free]), spare
        for i in free:
            more = min(reach - counts[i], max(1, remaining * weights[i] // pool), spare)
            counts[i] = counts[i] + more
            spare = spare - more
    return np.array([reach] + counts)


def uneven(key, amount, total, reach, skew):
    if amount == 2:
        one = jax.random.randint(key, (), max(1, total - reach), min(reach, total - 1) + 1)
        return jnp.stack([one, total - one])
    sizes = jnp.asarray(length_profile(amount, total, reach, skew), jnp.int32)
    couples = (amount - 1) // 2
    source_of, receiver = sizes[1:1 + 2 * couples:2], sizes[2:2 + 2 * couples:2]
    room = jnp.minimum(source_of - 1, reach - receiver)
    passed = jax.random.randint(jax.random.fold_in(key, 1), (couples,), 0, 1 << 20) % (room + 1)
    sizes = sizes.at[1:1 + 2 * couples:2].set(source_of - passed).at[2:2 + 2 * couples:2].set(receiver + passed)
    return sizes[jax.random.permutation(jax.random.fold_in(key, 2), amount)]


def centred(own_key, dims, spread, most, split=(), held_as=jnp.bfloat16):
    array = jax.random.normal(own_key, dims, jnp.float32) * spread
    if len(split) > 0:
        array = levels(own_key, dims, split, -0.22, 0.18) * array
    return jnp.clip(array, min=-most, max=most).astype(held_as)


def setup_inputs(seed: int = 0) -> dict:
    streams_of = jax.random.split(jax.random.key(seed), 11)
    queries = centred(streams_of[0], (REQUESTS, SUF_MAX, HEADS, HD), 1.0, 6.0, ((0, 32), (2, 8)))
    suffix_kv = centred(streams_of[1], (REQUESTS, SUF_MAX, KVH, 2 * HD), 1.0, 6.0, ((0, 32), (2, 8)))
    prefix_kv = centred(streams_of[2], (N_REQ, PREFIX, KVH, 2 * HD), 1.0, 6.0, ((0, 32), (2, 8)))
    out_weight = centred(streams_of[3], (HEADS * HD, D), (HEADS * HD) ** -0.5, 0.09375, ((0, 8),))
    residual = centred(streams_of[4], (REQUESTS, SUF_MAX, D), 1.0, 6.0, ((0, 32), (2, 8)))
    norm_gain = jnp.clip(1.0 + 0.1 * jax.random.normal(streams_of[5], (D,), jnp.float32), 0.5, 1.5)
    suffix_len = uneven(streams_of[6], REQUESTS, REQUESTS * SUF_MAX // 2, SUF_MAX, 2).astype(jnp.int32)
    member = jax.random.permutation(streams_of[7], REQUESTS).astype(jnp.int32)
    owner = draw_owner(jax.random.fold_in(streams_of[10], 71), 0)
    assign = jax.random.permutation(streams_of[9], REQUESTS).astype(jnp.int32)
    return {"queries": queries, "suffix_kv": suffix_kv, "prefix_kv": prefix_kv, "out_weight": out_weight, "residual": residual, "norm_gain": norm_gain, "suffix_len": suffix_len, "member": member, "owner": owner, "assign": assign}


def reference(queries, suffix_kv, prefix_kv, out_weight, residual, norm_gain, suffix_len, member, owner, assign):
    group_size = REQUESTS // GROUPS
    repeats = HEADS // KVH
    positions = jnp.arange(SUF_MAX)
    causal = positions[None, :] <= positions[:, None]
    stacked_weight = out_weight.astype(jnp.float32).reshape(N_TP, HEADS * HD // N_TP, D)

    def one_slot(slot):
        request = assign[slot]
        length = suffix_len[request]
        group = member[request] // group_size
        prefix_slab = lax.dynamic_index_in_dim(prefix_kv, owner[group], 0, keepdims=False)
        keys = jnp.concatenate([prefix_slab, suffix_kv[slot]], 0).astype(jnp.float32)
        query = queries[slot].astype(jnp.float32).reshape(SUF_MAX, KVH, repeats, HD)
        scores = jnp.einsum('sgrd,kgd->grsk', query, keys[..., :HD]) * 0.0625
        capped = 50.0 * jnp.tanh(scores / 50.0)
        allowed = jnp.concatenate([jnp.ones((SUF_MAX, PREFIX), bool), causal & (positions[None, :] < length)], 1)
        weights = jnp.where(allowed, jnp.exp(capped), jnp.float32(0.0))
        total = lax.optimization_barrier(jnp.sum(weights, -1))
        rounded = lax.optimization_barrier(weights.astype(jnp.bfloat16))
        numer = jnp.einsum('grsk,kgd->sgrd', rounded.astype(jnp.float32), keys[..., HD:])
        attended = (numer / jnp.moveaxis(total, 2, 0)[..., None]).astype(jnp.bfloat16)
        attended = lax.optimization_barrier(attended).astype(jnp.float32).reshape(SUF_MAX, N_TP, HEADS * HD // N_TP)
        partial_value = jnp.einsum('snk,nkd->snd', attended, stacked_weight)
        partial_value = lax.optimization_barrier(partial_value.astype(jnp.bfloat16)).astype(jnp.float32)
        projected = lax.optimization_barrier(jnp.sum(partial_value, 1))
        scale = lax.rsqrt(lax.optimization_barrier(jnp.mean(projected * projected, -1, keepdims=True)) + 1e-06)
        return (residual[slot].astype(jnp.float32) + projected * scale * norm_gain).astype(jnp.bfloat16)
    return lax.map(one_slot, jnp.arange(REQUESTS))
```

```python
import jax
import jax.numpy as jnp
from jax import lax
from jax.experimental import pallas as pl
from jax.experimental.pallas import tpu as pltpu
from jax.sharding import PartitionSpec as P

D = 3584
MESH = pl.DeviceIdType.MESH
CHUNKS = 4
PLANE = 16
ROWS = 1024 // PLANE // CHUNKS
BF = jnp.bfloat16
F32 = jnp.float32
NT = (((1,), (1,)), ((), ()))
COLS = 448


def kernel(
    suffix_len, member, owner, assign,
    q_hbm, suf_hbm, pre_hbm, w_hbm, res_hbm, gain_hbm,
    out,
    got, both, out_kv, kv,
    q, suf, w, wt, wtr, res, gain, acc, tot, att, attr,
    part, mid, own, landed, sq, sqr, table,
    local_sem, own_sem, p1s, p1r, zs, zr, p2s, p2r, ws, wr, ats, atr, rs, rr, ss, sr,
):
    req = lax.axis_index("req")
    tp = lax.axis_index("tp")
    half = req // PLANE
    me = req % PLANE
    mx, my = me % 4, me // 4
    z, core = tp // 2, tp % 2
    other_half = 1 - half
    partner = tp + 1 - 2 * core
    base = half * PLANE

    def away(d):
        return (my + d // 4) % 4 * 4 + (mx + d % 4) % 4

    def local(i, src, dst):
        return pltpu.make_async_copy(src, dst, local_sem.at[i])

    loads = [
        local(0, q_hbm, q), local(1, suf_hbm, suf), local(2, w_hbm, w),
        local(3, res_hbm, res), local(4, gain_hbm, gain),
    ]

    barrier = pltpu.get_barrier_semaphore()

    @pl.loop(1, PLANE)
    def _(d):
        pl.semaphore_signal(barrier, inc=1, device_id=(base + away(d), tp), device_id_type=MESH)

    @pl.loop(1, 8)
    def _(d):
        pl.semaphore_signal(barrier, inc=1, device_id=(req, (tp + d) % 8), device_id_type=MESH)

    pl.semaphore_signal(
        barrier, inc=1, device_id=(other_half * PLANE + me, tp), device_id_type=MESH
    )
    for load in loads:
        load.start()
    mine = [
        pltpu.make_async_copy(pre_hbm.at[me, c], got[c].at[me], own_sem.at[c])
        for c in range(CHUNKS)
    ]
    for copy in mine:
        copy.start()
    pl.semaphore_wait(barrier, 23)

    def first(c, d):
        to = away(d)
        return pltpu.make_async_remote_copy(
            src_ref=pre_hbm.at[to, c], dst_ref=got[c].at[me],
            send_sem=p1s.at[c, d], recv_sem=p1r.at[c, d],
            device_id=(base + to, tp), device_id_type=MESH,
        )

    for c in range(CHUNKS):
        @pl.loop(1, PLANE)
        def _(d, c=c):
            first(c, d).start()

    @pl.loop(0, PLANE)
    def _(d):
        for s in range(2):
            group = member[assign[(base + away(d)) * 2 + s]] // 8
            apart = owner[group] // PLANE - half
            table[2 * d + s] = group + 8 * apart * apart

    def across(c):
        return pltpu.make_async_remote_copy(
            src_ref=both[c].at[pl.ds(0, 8)], dst_ref=both[c].at[pl.ds(8, 8)],
            send_sem=zs.at[c], recv_sem=zr.at[c],
            device_id=(other_half * PLANE + me, tp), device_id_type=MESH,
        )

    def send_across(c):
        mine[c].wait()

        @pl.loop(1, PLANE)
        def _(d):
            first(c, d).wait_recv()

        for g in range(8):
            both[c][g] = got[c][owner[g] % PLANE]
        across(c).start()

    def third(c, s, d):
        return pltpu.make_async_remote_copy(
            src_ref=out_kv[c][s].at[d], dst_ref=kv[c][s].at[me],
            send_sem=p2s.at[c, s, d], recv_sem=p2r.at[c, s, d],
            device_id=(base + away(d), tp), device_id_type=MESH,
        )

    def send_needed(c):
        across(c).wait_recv()
        for s in range(2):
            kv[c][s][me] = both[c][table[s]]

            @pl.loop(1, PLANE)
            def _(d, s=s):
                out_kv[c][s][d] = both[c][table[2 * d + s]]

            @pl.loop(1, PLANE)
            def _(d, s=s):
                third(c, s, d).start()

    def weigh(s, keys):
        scores = lax.dot_general(q[s], keys, NT, preferred_element_type=F32)
        return jnp.exp(50.0 * jnp.tanh(scores * 0.00125))

    def lanes(weights):
        total = weights[:, :128]
        for i in range(1, weights.shape[1] // 128):
            total = total + weights[:, 128 * i : 128 * (i + 1)]
        return total

    def attend_suffix(s):
        length = suffix_len[assign[req * 2 + s]]
        row = lax.broadcasted_iota(jnp.int32, (512, 256), 0) % 256
        key = lax.broadcasted_iota(jnp.int32, (512, 256), 1)
        weights = weigh(s, suf[s, :, :256])
        weights = jnp.where((key <= row) & (key < length), weights, 0.0)
        acc[s] = jnp.dot(weights.astype(BF), suf[s, :, 256:], preferred_element_type=F32)
        tot[s] = lanes(weights)

    def attend(c, s):
        @pl.loop(1, PLANE)
        def _(d):
            third(c, s, d).wait_recv()

        both_parts = kv[c][s][...].reshape(PLANE * ROWS, 512)
        weights = weigh(s, both_parts[:, :256])
        acc[s] += jnp.dot(weights.astype(BF), both_parts[:, 256:], preferred_element_type=F32)
        tot[s] += lanes(weights)

    def to_partner(i):
        return pltpu.make_async_remote_copy(
            src_ref=wt.at[pl.ds(pl.multiple_of(896 * i + COLS * (1 - core), 64), COLS)],
            dst_ref=wtr.at[pl.ds(COLS * i, COLS)],
            send_sem=ws.at[i], recv_sem=wr.at[i],
            device_id=(req, partner), device_id_type=MESH,
        )

    def turn_weights():
        loads[2].wait()
        for i in range(4):
            wt[896 * i : 896 * (i + 1), :] = w[:, 896 * i : 896 * (i + 1)].T
        for i in range(4):
            to_partner(i).start()

    def share(s):
        return pltpu.make_async_remote_copy(
            src_ref=att.at[s], dst_ref=attr.at[s], send_sem=ats.at[s], recv_sem=atr.at[s],
            device_id=(req, partner), device_id_type=MESH,
        )

    near, far, cross = z + 1 - 2 * (z % 2), (z + 2) % 4, 3 - z
    middle = ((z + 1) // 2) % 2
    ahead = near + middle * (cross - near)

    def to_near(s):
        return pltpu.make_async_remote_copy(
            src_ref=part.at[s, 1], dst_ref=landed.at[s, 1],
            send_sem=rs.at[s, 1], recv_sem=rr.at[s, 1],
            device_id=(req, 2 * near + core), device_id_type=MESH,
        )

    def to_far(s):
        return pltpu.make_async_remote_copy(
            src_ref=part.at[s, 2], dst_ref=landed.at[s, 2],
            send_sem=rs.at[s, 2], recv_sem=rr.at[s, 2],
            device_id=(req, 2 * far + core), device_id_type=MESH,
        )

    def to_ahead(s):
        return pltpu.make_async_remote_copy(
            src_ref=part.at[s, 0], dst_ref=landed.at[s, 3 * middle],
            send_sem=rs.at[s, 0], recv_sem=rr.at[s, 3 * middle],
            device_id=(req, 2 * ahead + core), device_id_type=MESH,
        )

    def arrived(s, i):
        return pltpu.make_async_remote_copy(
            src_ref=part.at[s, 0], dst_ref=landed.at[s, i],
            send_sem=rs.at[s, 0], recv_sem=rr.at[s, i],
            device_id=(req, 2 * near + core), device_id_type=MESH,
        )

    def project(s):
        total = jnp.sum(tot[s], axis=1, keepdims=True)
        value = (acc[s] / total).astype(BF)
        att[s, :, :256] = value[:256]
        att[s, :, 256:] = value[256:]
        share(s).start()

        def here(block):
            start = pl.multiple_of(896 * block + COLS * core, 64)
            return lax.dot_general(
                wt[pl.ds(start, COLS), :], att[s], NT, preferred_element_type=F32
            )

        def there(block):
            start = pl.multiple_of(COLS * block, 64)
            return lax.dot_general(
                wtr[pl.ds(start, COLS), :], attr[s], NT, preferred_element_type=F32
            )

        own[s] = here(cross)
        mid[s] = here(far)
        share(s).wait_recv()
        part[s, 0] = (own[s] + there(cross)).astype(BF)
        to_ahead(s).start()
        mid[s] += there(far)

        @pl.when(middle == 0)
        def _():
            part[s, 2] = mid[s].astype(BF)
            to_far(s).start()

        part[s, 1] = (here(near) + there(near)).astype(BF)
        to_near(s).start()
        own[s] = here(z) + there(z)

        @pl.when(middle == 1)
        def _():
            arrived(s, 0).wait_recv()
            part[s, 2] = (mid[s] + landed[s, 0].astype(F32)).astype(BF)
            to_far(s).start()

    def tell(s, d):
        return pltpu.make_async_remote_copy(
            src_ref=sq.at[s], dst_ref=sqr.at[s, d], send_sem=ss.at[s, d], recv_sem=sr.at[s, d],
            device_id=(req, (tp + d) % 8), device_id_type=MESH,
        )

    def gather_sums(s):
        @pl.when(middle == 1)
        def _():
            arrived(s, 3).wait_recv()
            own[s] += landed[s, 3].astype(F32)

        to_near(s).wait_recv()
        to_far(s).wait_recv()
        value = own[s] + landed[s, 1].astype(F32) + landed[s, 2].astype(F32)
        own[s] = value
        sq[s] = jnp.broadcast_to(jnp.sum(value * value, axis=0, keepdims=True), (8, 256))

        @pl.loop(1, 8)
        def _(d):
            tell(s, d).start()

    def finish(s):
        @pl.loop(1, 8)
        def _(d):
            tell(s, d).wait_recv()

        squares = sq[s]
        for d in range(1, 8):
            squares = squares + sqr[s, d]
        scale = lax.rsqrt(squares[:1] / D + 1e-06)
        out[s] = (res[s].astype(F32) + own[s] * scale * gain[...]).astype(BF)

    loads[0].wait()
    loads[1].wait()
    attend_suffix(0)
    send_across(0)
    attend_suffix(1)
    send_across(1)
    turn_weights()
    send_across(2)
    send_needed(0)
    send_across(3)
    send_needed(1)
    attend(0, 0)
    attend(0, 1)
    send_needed(2)
    attend(1, 0)
    attend(1, 1)
    send_needed(3)
    attend(2, 0)
    attend(2, 1)
    for i in range(4):
        to_partner(i).wait_recv()
    attend(3, 0)
    project(0)
    attend(3, 1)
    project(1)
    loads[3].wait()
    loads[4].wait()
    gather_sums(0)
    finish(0)
    gather_sums(1)
    finish(1)

    for c in range(CHUNKS):
        across(c).wait_send()

        @pl.loop(1, PLANE)
        def _(d, c=c):
            first(c, d).wait_send()
            third(c, 0, d).wait_send()
            third(c, 1, d).wait_send()

    for i in range(4):
        to_partner(i).wait_send()
    for s in range(2):
        share(s).wait_send()
        to_near(s).wait_send()
        to_far(s).wait_send()
        to_ahead(s).wait_send()

        @pl.loop(1, 8)
        def _(d, s=s):
            tell(s, d).wait_send()


def local(
    queries, suffix_kv, prefix_kv, out_weight, residual, norm_gain, suffix_len, member, owner, assign
):
    query = jnp.transpose(queries, (0, 2, 1, 3)).reshape(2, 512, 256)
    suffix = suffix_kv.reshape(2, 256, 512)
    prefix = prefix_kv.reshape(PLANE, CHUNKS, ROWS, 512)
    stream = jnp.transpose(residual, (0, 2, 1))
    gain = jnp.broadcast_to(norm_gain[:, None], (COLS, 256))
    smem = pl.BlockSpec(memory_space=pltpu.SMEM)
    anywhere = pl.BlockSpec(memory_space=pl.ANY)
    V = pltpu.VMEM
    DMA = pltpu.SemaphoreType.DMA
    piece = V((PLANE, ROWS, 512), BF)
    pair = [[piece, piece] for _ in range(CHUNKS)]
    out = pl.pallas_call(
        kernel,
        name="prefill",
        out_shape=jax.ShapeDtypeStruct((2, COLS, 256), BF),
        in_specs=[smem] * 4 + [anywhere] * 6,
        out_specs=pl.BlockSpec(memory_space=pltpu.VMEM),
        scratch_shapes=[
            [piece] * CHUNKS, [piece] * CHUNKS, pair, pair,
            V((2, 512, 256), BF), V((2, 256, 512), BF), V((512, D), BF), V((D, 512), BF),
            V((D // 2, 512), BF), V((2, COLS, 256), BF), V((COLS, 256), F32),
            V((2, 512, 256), F32), V((2, 512, 128), F32), V((2, 256, 512), BF), V((2, 256, 512), BF),
            V((2, 3, COLS, 256), BF), V((2, COLS, 256), F32), V((2, COLS, 256), F32),
            V((2, 4, COLS, 256), BF), V((2, 8, 256), F32), V((2, 8, 8, 256), F32),
            pltpu.SMEM((2 * PLANE,), jnp.int32),
            DMA((5,)), DMA((CHUNKS,)), DMA((CHUNKS, PLANE)), DMA((CHUNKS, PLANE)),
            DMA((CHUNKS,)), DMA((CHUNKS,)), DMA((CHUNKS, 2, PLANE)), DMA((CHUNKS, 2, PLANE)),
            DMA((4,)), DMA((4,)), DMA((2,)), DMA((2,)), DMA((2, 3)), DMA((2, 4)),
            DMA((2, 8)), DMA((2, 8)),
        ],
        compiler_params=pltpu.CompilerParams(
            collective_id=0, has_side_effects=True, vmem_limit_bytes=56 * 2**20
        ),
    )(suffix_len, member, owner, assign, query, suffix, prefix, out_weight, stream, gain)
    return jnp.transpose(out, (0, 2, 1))


def solution(mesh):
    in_specs = (
        P("req", None, "tp", None),
        P("req", None, "tp", None),
        P("req", None, "tp", None),
        P("tp", None),
        P("req", None, "tp"),
        P("tp"),
        P(),
        P(),
        P(),
        P(),
    )
    out_specs = P("req", None, "tp")
    return jax.shard_map(local, mesh=mesh, in_specs=in_specs, out_specs=out_specs, check_vma=False)
```

```python
import jax
import jax.numpy as jnp
from jax import lax
from jax.experimental import pallas as pl
from jax.experimental.pallas import tpu as pltpu
from jax.sharding import PartitionSpec as P

D = 3584
MESH = pl.DeviceIdType.MESH
PLANE = 16
STEPS = [
    (0, 0), (2, 2), (2, 1), (1, 2), (2, 3), (3, 2), (1, 1), (3, 3),
    (1, 3), (3, 1), (2, 0), (0, 2), (1, 0), (0, 1), (3, 0), (0, 3),
]
CHUNKS = [(0, 16), (16, 16), (32, 16), (48, 16)]
LAST = len(CHUNKS) - 1
BF = jnp.bfloat16
F32 = jnp.float32
NT = (((1,), (1,)), ((), ()))
COLS = 448


def kernel(
    suffix_len, member, owner, assign,
    q_hbm, suf_hbm, pre_hbm, w_hbm, res_hbm, gain_hbm,
    out,
    got, both, out_kv, kv,
    raw, q, suf, w, wt, wtr, res, gain_row, gain, acc, tot, att, attr,
    part, mid, own, landed, sq, sqr, table,
    local_sem, own_sem, p1s, p1r, zs, zr, p2s, p2r, ws, wr, ats, atr, rs, rr, ss, sr,
):
    req = lax.axis_index("req")
    tp = lax.axis_index("tp")
    half = req // PLANE
    me = req % PLANE
    mx, my = me % 4, me // 4
    z, core = tp // 2, tp % 2
    other_half = 1 - half
    partner = tp + 1 - 2 * core
    base = half * PLANE

    peers = [(my + dy) % 4 * 4 + (mx + dx) % 4 for dx, dy in STEPS]

    def local(i, src, dst):
        return pltpu.make_async_copy(src, dst, local_sem.at[i])

    loads = [
        local(0, q_hbm, raw), local(1, suf_hbm, suf), local(2, w_hbm, w),
        local(3, res_hbm, res), local(4, gain_hbm, gain_row),
    ]

    barrier = pltpu.get_barrier_semaphore()

    pl.semaphore_signal(
        barrier, inc=1, device_id=(other_half * PLANE + me, tp), device_id_type=MESH
    )
    for d in range(1, PLANE):
        pl.semaphore_signal(barrier, inc=1, device_id=(base + peers[d], tp), device_id_type=MESH)
    for d in range(1, 8):
        pl.semaphore_signal(barrier, inc=1, device_id=(req, (tp + d) % 8), device_id_type=MESH)
    for load in loads:
        load.start()
    def span(c):
        return pl.ds(*CHUNKS[c])

    mine = [
        pltpu.make_async_copy(pre_hbm.at[me, span(k)], got[k].at[me], own_sem.at[k])
        for k in range(len(CHUNKS))
    ]
    for copy in mine:
        copy.start()
    pl.semaphore_wait(barrier, 23)

    def first(k, d):
        return pltpu.make_async_remote_copy(
            src_ref=pre_hbm.at[peers[d], span(k)], dst_ref=got[k].at[me],
            send_sem=p1s.at[k, d], recv_sem=p1r.at[k, d],
            device_id=(base + peers[d], tp), device_id_type=MESH,
        )

    for k in range(len(CHUNKS)):
        for d in range(1, PLANE):
            first(k, d).start()

    for d in range(PLANE):
        for s in range(2):
            group = member[assign[(base + peers[d]) * 2 + s]] // 8
            apart = owner[group] // PLANE - half
            table[2 * d + s] = group + 8 * apart * apart

    def across(c):
        return pltpu.make_async_remote_copy(
            src_ref=both[c].at[pl.ds(0, 8)], dst_ref=both[c].at[pl.ds(8, 8)],
            send_sem=zs.at[c], recv_sem=zr.at[c],
            device_id=(other_half * PLANE + me, tp), device_id_type=MESH,
        )

    def send_across(c):
        mine[c].wait()
        for d in range(1, PLANE):
            first(c, d).wait_recv()
        for g in range(8):
            both[c][g] = got[c][owner[g] % PLANE]
        across(c).start()

    def third(c, s, d):
        return pltpu.make_async_remote_copy(
            src_ref=out_kv[c][s].at[d], dst_ref=kv[c][s].at[me],
            send_sem=p2s.at[c, s, d], recv_sem=p2r.at[c, s, d],
            device_id=(base + peers[d], tp), device_id_type=MESH,
        )

    def place(c, s):
        return (s, 0) if c == LAST else (0, s * CHUNKS[c][1])

    def send_needed(c):
        across(c).wait_recv()
        for s in range(2):
            i, row = place(c, s)
            kv[c][i][me, row : row + CHUNKS[c][1]] = both[c][table[s]]
            for d in range(1, PLANE):
                out_kv[c][i][d, row : row + CHUNKS[c][1]] = both[c][table[2 * d + s]]
            if s == 1 or i == s and c == LAST:
                for d in range(1, PLANE):
                    third(c, i, d).start()

    def weigh(s, keys):
        scores = lax.dot_general(q[s], keys, NT, preferred_element_type=F32)
        return jnp.exp(50.0 * jnp.tanh(scores * 0.00125))

    def lanes(weights):
        total = weights[:, :128]
        for i in range(1, weights.shape[1] // 128):
            total = total + weights[:, 128 * i : 128 * (i + 1)]
        return total

    def attend_suffix(s):
        length = suffix_len[assign[req * 2 + s]]
        row = lax.broadcasted_iota(jnp.int32, (512, 256), 0) % 256
        key = lax.broadcasted_iota(jnp.int32, (512, 256), 1)
        weights = weigh(s, suf[s, :, :256])
        weights = jnp.where((key <= row) & (key < length), weights, 0.0)
        acc[s] = jnp.dot(weights.astype(BF), suf[s, :, 256:], preferred_element_type=F32)
        tot[s] = lanes(weights)

    def attend(c, s):
        i, row = place(c, s)
        if i == s:
            for d in range(1, PLANE):
                third(c, i, d).wait_recv()

        both_parts = kv[c][i][:, row : row + CHUNKS[c][1]].reshape(-1, 512)
        weights = weigh(s, both_parts[:, :256])
        acc[s] += jnp.dot(weights.astype(BF), both_parts[:, 256:], preferred_element_type=F32)
        tot[s] += lanes(weights)

    def to_partner(i):
        return pltpu.make_async_remote_copy(
            src_ref=wt.at[pl.ds(pl.multiple_of(896 * i + COLS * (1 - core), 64), COLS)],
            dst_ref=wtr.at[pl.ds(COLS * i, COLS)],
            send_sem=ws.at[i], recv_sem=wr.at[i],
            device_id=(req, partner), device_id_type=MESH,
        )

    def turn_weights(i):
        if i == 0:
            loads[2].wait()
        wt[896 * i : 896 * (i + 1), :] = w[:, 896 * i : 896 * (i + 1)].T
        to_partner(i).start()

    def share(s):
        return pltpu.make_async_remote_copy(
            src_ref=att.at[s], dst_ref=attr.at[s], send_sem=ats.at[s], recv_sem=atr.at[s],
            device_id=(req, partner), device_id_type=MESH,
        )

    near, far, cross = z + 1 - 2 * (z % 2), (z + 2) % 4, 3 - z
    middle = ((z + 1) // 2) % 2
    ahead = near + middle * (cross - near)

    def to_near(s):
        return pltpu.make_async_remote_copy(
            src_ref=part.at[s, 1], dst_ref=landed.at[s, 1],
            send_sem=rs.at[s, 1], recv_sem=rr.at[s, 1],
            device_id=(req, 2 * near + core), device_id_type=MESH,
        )

    def to_far(s):
        return pltpu.make_async_remote_copy(
            src_ref=part.at[s, 2], dst_ref=landed.at[s, 2],
            send_sem=rs.at[s, 2], recv_sem=rr.at[s, 2],
            device_id=(req, 2 * far + core), device_id_type=MESH,
        )

    def to_ahead(s):
        return pltpu.make_async_remote_copy(
            src_ref=part.at[s, 0], dst_ref=landed.at[s, 3 * middle],
            send_sem=rs.at[s, 0], recv_sem=rr.at[s, 3 * middle],
            device_id=(req, 2 * ahead + core), device_id_type=MESH,
        )

    def arrived(s, i):
        return pltpu.make_async_remote_copy(
            src_ref=part.at[s, 0], dst_ref=landed.at[s, i],
            send_sem=rs.at[s, 0], recv_sem=rr.at[s, i],
            device_id=(req, 2 * near + core), device_id_type=MESH,
        )

    def project(s):
        total = jnp.sum(tot[s], axis=1, keepdims=True)
        value = (acc[s] / total).astype(BF)
        att[s, :, :256] = value[:256]
        att[s, :, 256:] = value[256:]
        share(s).start()

        def here(block):
            start = pl.multiple_of(896 * block + COLS * core, 64)
            return lax.dot_general(
                wt[pl.ds(start, COLS), :], att[s], NT, preferred_element_type=F32
            )

        def there(block):
            start = pl.multiple_of(COLS * block, 64)
            return lax.dot_general(
                wtr[pl.ds(start, COLS), :], attr[s], NT, preferred_element_type=F32
            )

        own[s] = here(cross)
        mid[s] = here(far)
        share(s).wait_recv()
        part[s, 0] = (own[s] + there(cross)).astype(BF)
        to_ahead(s).start()
        mid[s] += there(far)

        @pl.when(middle == 0)
        def _():
            part[s, 2] = mid[s].astype(BF)
            to_far(s).start()

        part[s, 1] = (here(near) + there(near)).astype(BF)
        to_near(s).start()
        own[s] = here(z) + there(z)

        @pl.when(middle == 1)
        def _():
            arrived(s, 0).wait_recv()
            part[s, 2] = (mid[s] + landed[s, 0].astype(F32)).astype(BF)
            to_far(s).start()

    def tell(s, d):
        return pltpu.make_async_remote_copy(
            src_ref=sq.at[s], dst_ref=sqr.at[s, d], send_sem=ss.at[s, d], recv_sem=sr.at[s, d],
            device_id=(req, (tp + d) % 8), device_id_type=MESH,
        )

    def gather_sums(s):
        @pl.when(middle == 1)
        def _():
            arrived(s, 3).wait_recv()
            own[s] += landed[s, 3].astype(F32)

        to_near(s).wait_recv()
        to_far(s).wait_recv()
        value = own[s] + landed[s, 1].astype(F32) + landed[s, 2].astype(F32)
        own[s] = value
        sq[s] = jnp.sum(value * value, axis=0, keepdims=True)

        @pl.loop(1, 8)
        def _(d):
            tell(s, d).start()

    def finish(s):
        @pl.loop(1, 8)
        def _(d):
            tell(s, d).wait_recv()

        squares = sq[s]
        for d in range(1, 8):
            squares = squares + sqr[s, d]
        scale = lax.rsqrt(squares / D + 1e-06)
        out[s] = (res[s].astype(F32) + own[s] * scale * gain[...]).astype(BF)

    loads[0].wait()
    for s in range(2):
        for h in range(2):
            q[s, 256 * h : 256 * (h + 1)] = raw[s, :, h, :]
    loads[4].wait()
    gain[...] = jnp.broadcast_to(gain_row[...][None, :], (256, COLS)).T
    loads[1].wait()
    attend_suffix(0)
    attend_suffix(1)
    for c in range(LAST + 1):
        send_across(c)
        for i in range(4):
            if min(i, LAST) == c:
                turn_weights(i)
    for c in range(LAST + 1):
        send_needed(c)
        if c >= 1:
            attend(c - 1, 0)
            attend(c - 1, 1)
    for i in range(4):
        to_partner(i).wait_recv()
    attend(LAST, 0)
    project(0)
    attend(LAST, 1)
    project(1)
    for c in range(len(CHUNKS)):
        across(c).wait_send()
        for i in range(2 if c == LAST else 1):
            for d in range(1, PLANE):
                third(c, i, d).wait_send()
    for k in range(len(CHUNKS)):
        for d in range(1, PLANE):
            first(k, d).wait_send()
    loads[3].wait()
    gather_sums(0)
    finish(0)
    gather_sums(1)
    finish(1)

    for i in range(4):
        to_partner(i).wait_send()
    for s in range(2):
        share(s).wait_send()
        to_near(s).wait_send()
        to_far(s).wait_send()
        to_ahead(s).wait_send()

        @pl.loop(1, 8)
        def _(d, s=s):
            tell(s, d).wait_send()


def local(
    queries, suffix_kv, prefix_kv, out_weight, residual, norm_gain, suffix_len, member, owner, assign
):
    suffix = suffix_kv.reshape(2, 256, 512)
    prefix = prefix_kv.reshape(PLANE, -1, 512)
    stream = jnp.transpose(residual, (0, 2, 1))
    smem = pl.BlockSpec(memory_space=pltpu.SMEM)
    anywhere = pl.BlockSpec(memory_space=pl.ANY)
    V = pltpu.VMEM
    DMA = pltpu.SemaphoreType.DMA

    def piece(rows):
        return V((PLANE, rows, 512), BF)

    pieces = [piece(rows) for _, rows in CHUNKS]
    pair = [[piece(2 * rows)] for _, rows in CHUNKS[:-1]] + [[pieces[-1]] * 2]
    out = pl.pallas_call(
        kernel,
        name="prefill",
        out_shape=jax.ShapeDtypeStruct((2, COLS, 256), BF),
        in_specs=[smem] * 4 + [anywhere] * 6,
        out_specs=pl.BlockSpec(memory_space=pltpu.VMEM),
        scratch_shapes=[
            pieces, pieces, pair, pair,
            V((2, 256, 2, 256), BF), V((2, 512, 256), BF), V((2, 256, 512), BF), V((512, D), BF), V((D, 512), BF),
            V((D // 2, 512), BF), V((2, COLS, 256), BF), V((COLS,), F32), V((COLS, 256), F32),
            V((2, 512, 256), F32), V((2, 512, 128), F32), V((2, 256, 512), BF), V((2, 256, 512), BF),
            V((2, 3, COLS, 256), BF), V((2, COLS, 256), F32), V((2, COLS, 256), F32),
            V((2, 4, COLS, 256), BF), V((2, 1, 256), F32), V((2, 8, 1, 256), F32),
            pltpu.SMEM((2 * PLANE,), jnp.int32),
            DMA((5,)), DMA((LAST + 1,)), DMA((LAST + 1, PLANE)), DMA((LAST + 1, PLANE)),
            DMA((LAST + 1,)), DMA((LAST + 1,)), DMA((LAST + 1, 2, PLANE)), DMA((LAST + 1, 2, PLANE)),
            DMA((4,)), DMA((4,)), DMA((2,)), DMA((2,)), DMA((2, 3)), DMA((2, 4)),
            DMA((2, 8)), DMA((2, 8)),
        ],
        compiler_params=pltpu.CompilerParams(
            collective_id=0, has_side_effects=True, vmem_limit_bytes=56 * 2**20
        ),
    )(suffix_len, member, owner, assign, queries, suffix, prefix, out_weight, stream, norm_gain)
    return jnp.transpose(out, (0, 2, 1))


def solution(mesh):
    in_specs = (
        P("req", None, "tp", None),
        P("req", None, "tp", None),
        P("req", None, "tp", None),
        P("tp", None),
        P("req", None, "tp"),
        P("tp"),
        P(),
        P(),
        P(),
        P(),
    )
    out_specs = P("req", None, "tp")
    return jax.shard_map(local, mesh=mesh, in_specs=in_specs, out_specs=out_specs, check_vma=False)
```

```python
import jax
import jax.numpy as jnp
from jax import lax
from jax.experimental import pallas as pl
from jax.experimental.pallas import tpu as pltpu
from jax.sharding import PartitionSpec as P

D = 3584
MESH = pl.DeviceIdType.MESH
PLANE = 16
STEPS = [
    (0, 0), (2, 2), (2, 1), (1, 2), (2, 3), (3, 2), (1, 1), (3, 3),
    (1, 3), (3, 1), (2, 0), (0, 2), (1, 0), (0, 1), (3, 0), (0, 3),
]
CHUNKS = [(0, 16), (16, 16), (32, 16), (48, 16)]
LAST = len(CHUNKS) - 1
UNITS = [[(0, 0), (0, 1)], [(1, 0), (1, 1)], [(2, 0)], [(3, 0)], [(2, 1), (3, 1)]]
BF = jnp.bfloat16
F32 = jnp.float32
NT = (((1,), (1,)), ((), ()))
COLS = 448


def kernel(
    lens_hbm, member_hbm, owner_hbm, assign_hbm,
    q_hbm, suf_hbm, pre_hbm, w_hbm, res_hbm, gain_hbm,
    out_hbm,
    got, both, out_kv, kv,
    suffix_len, member, owner, assign, out, raw, q, suf, w, wt, wtr, res, gain_row, gain, acc, tot, att, attr,
    part, mid, own, landed, sq, sqr, table,
    local_sem, own_sem, p1s, p1r, zs, zr, p2s, p2r, ws, wr, ats, atr, rs, rr, ss, sr,
):
    req = lax.axis_index("req")
    tp = lax.axis_index("tp")
    half = req // PLANE
    me = req % PLANE
    mx, my = me % 4, me // 4
    z, core = tp // 2, tp % 2
    other_half = 1 - half
    partner = tp + 1 - 2 * core
    base = half * PLANE

    peers = [(my + dy) % 4 * 4 + (mx + dx) % 4 for dx, dy in STEPS]

    def local(i, src, dst):
        return pltpu.make_async_copy(src, dst, local_sem.at[i])

    loads = [
        local(0, q_hbm, raw), local(1, suf_hbm, suf), local(2, w_hbm, w),
        local(3, res_hbm, res), local(4, gain_hbm, gain_row),
        local(5, lens_hbm, suffix_len), local(6, member_hbm, member), local(7, owner_hbm, owner),
        local(8, assign_hbm, assign),
    ]

    barrier = pltpu.get_barrier_semaphore()

    pl.semaphore_signal(
        barrier, inc=1, device_id=(other_half * PLANE + me, tp), device_id_type=MESH
    )
    for d in range(1, PLANE):
        pl.semaphore_signal(barrier, inc=1, device_id=(base + peers[d], tp), device_id_type=MESH)
    for d in range(1, 8):
        pl.semaphore_signal(barrier, inc=1, device_id=(req, (tp + d) % 8), device_id_type=MESH)
    for load in loads:
        load.start()
    def span(c):
        return pl.ds(*CHUNKS[c])

    mine = [
        pltpu.make_async_copy(pre_hbm.at[me, span(k)], got[k].at[me], own_sem.at[k])
        for k in range(len(CHUNKS))
    ]
    for copy in mine:
        copy.start()
    pl.semaphore_wait(barrier, 23)

    def first(k, d):
        return pltpu.make_async_remote_copy(
            src_ref=pre_hbm.at[peers[d], span(k)], dst_ref=got[k].at[me],
            send_sem=p1s.at[k, d], recv_sem=p1r.at[k, d],
            device_id=(base + peers[d], tp), device_id_type=MESH,
        )

    for k in range(len(CHUNKS)):
        for d in range(1, PLANE):
            first(k, d).start()

    for load in loads[5:]:
        load.wait()

    for d in range(PLANE):
        for s in range(2):
            group = member[assign[(base + peers[d]) * 2 + s]] // 8
            apart = owner[group] // PLANE - half
            table[2 * d + s] = group + 8 * apart * apart

    def across(c):
        return pltpu.make_async_remote_copy(
            src_ref=both[c].at[pl.ds(0, 8)], dst_ref=both[c].at[pl.ds(8, 8)],
            send_sem=zs.at[c], recv_sem=zr.at[c],
            device_id=(other_half * PLANE + me, tp), device_id_type=MESH,
        )

    def send_across(c):
        mine[c].wait()
        for d in range(1, PLANE):
            first(c, d).wait_recv()
        for g in range(8):
            both[c][g] = got[c][owner[g] % PLANE]
        across(c).start()

    def third(u, d):
        return pltpu.make_async_remote_copy(
            src_ref=out_kv[u].at[d], dst_ref=kv[u].at[me],
            send_sem=p2s.at[u, d], recv_sem=p2r.at[u, d],
            device_id=(base + peers[d], tp), device_id_type=MESH,
        )

    def place(c, s):
        for u, parts in enumerate(UNITS):
            if (c, s) in parts:
                row = sum(CHUNKS[k][1] for k, _ in parts[: parts.index((c, s))])
                return u, slice(row, row + CHUNKS[c][1])

    def send_needed(c):
        across(c).wait_recv()
        for s in range(2):
            u, rows = place(c, s)
            kv[u][me, rows] = both[c][table[s]]
            for d in range(1, PLANE):
                out_kv[u][d, rows] = both[c][table[2 * d + s]]
            if UNITS[u][-1] == (c, s):
                for d in range(1, PLANE):
                    third(u, d).start()

    def weigh(s, keys):
        scores = lax.dot_general(q[s], keys, NT, preferred_element_type=F32)
        return jnp.exp(50.0 * jnp.tanh(scores * 0.00125))

    def lanes(weights):
        total = weights[:, :128]
        for i in range(1, weights.shape[1] // 128):
            total = total + weights[:, 128 * i : 128 * (i + 1)]
        return total

    def attend_suffix(s):
        length = suffix_len[assign[req * 2 + s]]
        row = lax.broadcasted_iota(jnp.int32, (512, 256), 0) % 256
        key = lax.broadcasted_iota(jnp.int32, (512, 256), 1)
        weights = weigh(s, suf[s, :, :256])
        weights = jnp.where((key <= row) & (key < length), weights, 0.0)
        acc[s] = jnp.dot(weights.astype(BF), suf[s, :, 256:], preferred_element_type=F32)
        tot[s] = lanes(weights)

    def attend(c, s):
        u, rows = place(c, s)
        if UNITS[u][0] == (c, s):
            for d in range(1, PLANE):
                third(u, d).wait_recv()

        both_parts = kv[u][:, rows].reshape(-1, 512)
        weights = weigh(s, both_parts[:, :256])
        acc[s] += jnp.dot(weights.astype(BF), both_parts[:, 256:], preferred_element_type=F32)
        tot[s] += lanes(weights)

    def to_partner(i):
        return pltpu.make_async_remote_copy(
            src_ref=wt.at[pl.ds(pl.multiple_of(896 * i + COLS * (1 - core), 64), COLS)],
            dst_ref=wtr.at[pl.ds(COLS * i, COLS)],
            send_sem=ws.at[i], recv_sem=wr.at[i],
            device_id=(req, partner), device_id_type=MESH,
        )

    def turn_weights(i):
        if i == 0:
            loads[2].wait()
        wt[896 * i : 896 * (i + 1), :] = w[:, 896 * i : 896 * (i + 1)].T
        to_partner(i).start()

    def share(s):
        return pltpu.make_async_remote_copy(
            src_ref=att.at[s], dst_ref=attr.at[s], send_sem=ats.at[s], recv_sem=atr.at[s],
            device_id=(req, partner), device_id_type=MESH,
        )

    near, far, cross = z + 1 - 2 * (z % 2), (z + 2) % 4, 3 - z
    middle = ((z + 1) // 2) % 2
    ahead = near + middle * (cross - near)

    def to_near(s):
        return pltpu.make_async_remote_copy(
            src_ref=part.at[s, 1], dst_ref=landed.at[s, 1],
            send_sem=rs.at[s, 1], recv_sem=rr.at[s, 1],
            device_id=(req, 2 * near + core), device_id_type=MESH,
        )

    def to_far(s):
        return pltpu.make_async_remote_copy(
            src_ref=part.at[s, 2], dst_ref=landed.at[s, 2],
            send_sem=rs.at[s, 2], recv_sem=rr.at[s, 2],
            device_id=(req, 2 * far + core), device_id_type=MESH,
        )

    def to_ahead(s):
        return pltpu.make_async_remote_copy(
            src_ref=part.at[s, 0], dst_ref=landed.at[s, 3 * middle],
            send_sem=rs.at[s, 0], recv_sem=rr.at[s, 3 * middle],
            device_id=(req, 2 * ahead + core), device_id_type=MESH,
        )

    def arrived(s, i):
        return pltpu.make_async_remote_copy(
            src_ref=part.at[s, 0], dst_ref=landed.at[s, i],
            send_sem=rs.at[s, 0], recv_sem=rr.at[s, i],
            device_id=(req, 2 * near + core), device_id_type=MESH,
        )

    def project(s):
        total = jnp.sum(tot[s], axis=1, keepdims=True)
        value = (acc[s] / total).astype(BF)
        att[s, :, :256] = value[:256]
        att[s, :, 256:] = value[256:]
        share(s).start()

        def here(block):
            start = pl.multiple_of(896 * block + COLS * core, 64)
            return lax.dot_general(
                wt[pl.ds(start, COLS), :], att[s], NT, preferred_element_type=F32
            )

        def there(block):
            start = pl.multiple_of(COLS * block, 64)
            return lax.dot_general(
                wtr[pl.ds(start, COLS), :], attr[s], NT, preferred_element_type=F32
            )

        own[s] = here(cross)
        mid[s] = here(far)
        share(s).wait_recv()
        part[s, 0] = (own[s] + there(cross)).astype(BF)
        to_ahead(s).start()
        mid[s] += there(far)

        @pl.when(middle == 0)
        def _():
            part[s, 2] = mid[s].astype(BF)
            to_far(s).start()

        part[s, 1] = (here(near) + there(near)).astype(BF)
        to_near(s).start()
        own[s] = here(z) + there(z)

        @pl.when(middle == 1)
        def _():
            arrived(s, 0).wait_recv()
            part[s, 2] = (mid[s] + landed[s, 0].astype(F32)).astype(BF)
            to_far(s).start()

    def tell(s, d):
        return pltpu.make_async_remote_copy(
            src_ref=sq.at[s], dst_ref=sqr.at[s, d], send_sem=ss.at[s, d], recv_sem=sr.at[s, d],
            device_id=(req, (tp + d) % 8), device_id_type=MESH,
        )

    def gather_sums(s):
        @pl.when(middle == 1)
        def _():
            arrived(s, 3).wait_recv()
            own[s] += landed[s, 3].astype(F32)

        to_near(s).wait_recv()
        to_far(s).wait_recv()
        value = own[s] + landed[s, 1].astype(F32) + landed[s, 2].astype(F32)
        own[s] = value
        sq[s] = jnp.sum(value * value, axis=0, keepdims=True)

        @pl.loop(1, 8)
        def _(d):
            tell(s, d).start()

    def finish(s):
        @pl.loop(1, 8)
        def _(d):
            tell(s, d).wait_recv()

        squares = sq[s]
        for d in range(1, 8):
            squares = squares + sqr[s, d]
        scale = lax.rsqrt(squares / D + 1e-06)
        out[s] = (res[s].astype(F32) + own[s] * scale * gain[...]).astype(BF)
        local(9 + s, out.at[s], out_hbm.at[s]).start()

    def prepare():
        loads[0].wait()
        for s in range(2):
            for h in range(2):
                q[s, 256 * h : 256 * (h + 1)] = raw[s, :, h, :]
        loads[4].wait()
        gain[...] = jnp.broadcast_to(gain_row[...][None, :], (256, COLS)).T
        loads[1].wait()

    prepare()
    attend_suffix(0)
    send_across(0)
    attend_suffix(1)
    send_across(1)
    turn_weights(0)
    send_across(2)
    turn_weights(1)
    send_across(3)
    send_needed(0)
    turn_weights(2)
    turn_weights(3)
    send_needed(1)
    attend(0, 0)
    attend(0, 1)
    send_needed(2)
    attend(1, 0)
    attend(1, 1)
    send_needed(3)
    attend(2, 0)
    for i in range(4):
        to_partner(i).wait_recv()
    attend(3, 0)
    project(0)
    attend(2, 1)
    attend(3, 1)
    project(1)
    for c in range(len(CHUNKS)):
        across(c).wait_send()
    for k in range(len(CHUNKS)):
        for d in range(1, PLANE):
            first(k, d).wait_send()
    for u in range(len(UNITS)):
        for d in range(1, PLANE):
            third(u, d).wait_send()
    loads[3].wait()
    gather_sums(0)
    finish(0)
    gather_sums(1)
    finish(1)

    for i in range(4):
        to_partner(i).wait_send()
    for s in range(2):
        share(s).wait_send()
        to_near(s).wait_send()
        to_far(s).wait_send()
        to_ahead(s).wait_send()

        @pl.loop(1, 8)
        def _(d, s=s):
            tell(s, d).wait_send()

        local(9 + s, out.at[s], out_hbm.at[s]).wait()


def local(
    queries, suffix_kv, prefix_kv, out_weight, residual, norm_gain, suffix_len, member, owner, assign
):
    suffix = suffix_kv.reshape(2, 256, 512)
    prefix = prefix_kv.reshape(PLANE, -1, 512)
    stream = jnp.transpose(residual, (0, 2, 1))
    anywhere = pl.BlockSpec(memory_space=pl.ANY)
    V = pltpu.VMEM
    DMA = pltpu.SemaphoreType.DMA

    def piece(rows):
        return V((PLANE, rows, 512), BF)

    pieces = [piece(rows) for _, rows in CHUNKS]
    units = [piece(sum(CHUNKS[c][1] for c, _ in parts)) for parts in UNITS]
    out = pl.pallas_call(
        kernel,
        name="prefill",
        out_shape=jax.ShapeDtypeStruct((2, COLS, 256), BF),
        in_specs=[anywhere] * 10,
        out_specs=anywhere,
        scratch_shapes=[
            pieces, pieces, units, units,
            pltpu.SMEM((64,), jnp.int32), pltpu.SMEM((64,), jnp.int32), pltpu.SMEM((8,), jnp.int32),
            pltpu.SMEM((64,), jnp.int32), V((2, COLS, 256), BF), V((2, 256, 2, 256), BF), V((2, 512, 256), BF), V((2, 256, 512), BF), V((512, D), BF), V((D, 512), BF),
            V((D // 2, 512), BF), V((2, COLS, 256), BF), V((COLS,), F32), V((COLS, 256), F32),
            V((2, 512, 256), F32), V((2, 512, 128), F32), V((2, 256, 512), BF), V((2, 256, 512), BF),
            V((2, 3, COLS, 256), BF), V((2, COLS, 256), F32), V((2, COLS, 256), F32),
            V((2, 4, COLS, 256), BF), V((2, 1, 256), F32), V((2, 8, 1, 256), F32),
            pltpu.SMEM((2 * PLANE,), jnp.int32),
            DMA((11,)), DMA((LAST + 1,)), DMA((LAST + 1, PLANE)), DMA((LAST + 1, PLANE)),
            DMA((LAST + 1,)), DMA((LAST + 1,)), DMA((len(UNITS), PLANE)), DMA((len(UNITS), PLANE)),
            DMA((4,)), DMA((4,)), DMA((2,)), DMA((2,)), DMA((2, 3)), DMA((2, 4)),
            DMA((2, 8)), DMA((2, 8)),
        ],
        compiler_params=pltpu.CompilerParams(
            collective_id=0, has_side_effects=True, vmem_limit_bytes=56 * 2**20
        ),
    )(suffix_len, member, owner, assign, queries, suffix, prefix, out_weight, stream, norm_gain)
    return jnp.transpose(out, (0, 2, 1))


def solution(mesh):
    in_specs = (
        P("req", None, "tp", None),
        P("req", None, "tp", None),
        P("req", None, "tp", None),
        P("tp", None),
        P("req", None, "tp"),
        P("tp"),
        P(),
        P(),
        P(),
        P(),
    )
    out_specs = P("req", None, "tp")
    return jax.shard_map(local, mesh=mesh, in_specs=in_specs, out_specs=out_specs, check_vma=False)
```

```python
import jax
import jax.numpy as jnp
from jax import lax
from jax.experimental import pallas as pl
from jax.experimental.pallas import tpu as pltpu
from jax.sharding import PartitionSpec as P

D = 3584
MESH = pl.DeviceIdType.MESH
PLANE = 16
STEPS = [
    (0, 0), (2, 2), (2, 1), (1, 2), (2, 3), (3, 2), (1, 1), (3, 3),
    (1, 3), (3, 1), (2, 0), (0, 2), (1, 0), (0, 1), (3, 0), (0, 3),
]
CHUNKS = [(0, 16), (16, 16), (32, 16), (48, 16)]
LAST = len(CHUNKS) - 1
UNITS = [[(0, 0), (0, 1)], [(1, 0), (1, 1)], [(2, 0)], [(3, 0)], [(2, 1), (3, 1)]]
BF = jnp.bfloat16
F32 = jnp.float32
NT = (((1,), (1,)), ((), ()))
COLS = 448


def kernel(
    lens_hbm, member_hbm, owner_hbm, assign_hbm,
    q_hbm, suf_hbm, pre_hbm, w_hbm, res_hbm, gain_hbm,
    out,
    got, both, out_kv, kv,
    suffix_len, member, owner, assign, raw, q, suf, w, wt, wtr, res, gain_row, gain, acc, tot, att, attr,
    part, mid, own, landed, sq, sqr, table,
    local_sem, own_sem, p1s, p1r, zs, zr, p2s, p2r, ws, wr, ats, atr, rs, rr, ss, sr,
):
    req = lax.axis_index("req")
    tp = lax.axis_index("tp")
    half = req // PLANE
    me = req % PLANE
    mx, my = me % 4, me // 4
    z, core = tp // 2, tp % 2
    other_half = 1 - half
    partner = tp + 1 - 2 * core
    base = half * PLANE

    peers = [(my + dy) % 4 * 4 + (mx + dx) % 4 for dx, dy in STEPS]

    def local(i, src, dst):
        return pltpu.make_async_copy(src, dst, local_sem.at[i])

    loads = [
        local(0, q_hbm, raw), local(1, suf_hbm, suf), local(2, w_hbm, w),
        local(3, res_hbm, res), local(4, gain_hbm, gain_row),
        local(5, lens_hbm, suffix_len), local(6, member_hbm, member), local(7, owner_hbm, owner),
        local(8, assign_hbm, assign),
    ]

    barrier = pltpu.get_barrier_semaphore()

    pl.semaphore_signal(
        barrier, inc=1, device_id=(other_half * PLANE + me, tp), device_id_type=MESH
    )
    for d in range(1, PLANE):
        pl.semaphore_signal(barrier, inc=1, device_id=(base + peers[d], tp), device_id_type=MESH)
    for d in range(1, 8):
        pl.semaphore_signal(barrier, inc=1, device_id=(req, (tp + d) % 8), device_id_type=MESH)
    for load in loads:
        load.start()
    def span(c):
        return pl.ds(*CHUNKS[c])

    mine = [
        pltpu.make_async_copy(pre_hbm.at[me, span(k)], got[k].at[me], own_sem.at[k])
        for k in range(len(CHUNKS))
    ]
    for copy in mine:
        copy.start()
    pl.semaphore_wait(barrier, 23)

    def first(k, d):
        return pltpu.make_async_remote_copy(
            src_ref=pre_hbm.at[peers[d], span(k)], dst_ref=got[k].at[me],
            send_sem=p1s.at[k, d], recv_sem=p1r.at[k, d],
            device_id=(base + peers[d], tp), device_id_type=MESH,
        )

    for k in range(len(CHUNKS)):
        for d in range(1, PLANE):
            first(k, d).start()

    for load in loads[5:]:
        load.wait()

    for d in range(PLANE):
        for s in range(2):
            group = member[assign[(base + peers[d]) * 2 + s]] // 8
            apart = owner[group] // PLANE - half
            table[2 * d + s] = group + 8 * apart * apart

    def across(c):
        return pltpu.make_async_remote_copy(
            src_ref=both[c].at[pl.ds(0, 8)], dst_ref=both[c].at[pl.ds(8, 8)],
            send_sem=zs.at[c], recv_sem=zr.at[c],
            device_id=(other_half * PLANE + me, tp), device_id_type=MESH,
        )

    def send_across(c):
        mine[c].wait()
        for d in range(1, PLANE):
            first(c, d).wait_recv()
        for g in range(8):
            both[c][g] = got[c][owner[g] % PLANE]
        across(c).start()

    def third(u, d):
        return pltpu.make_async_remote_copy(
            src_ref=out_kv[u].at[d], dst_ref=kv[u].at[me],
            send_sem=p2s.at[u, d], recv_sem=p2r.at[u, d],
            device_id=(base + peers[d], tp), device_id_type=MESH,
        )

    def place(c, s):
        for u, parts in enumerate(UNITS):
            if (c, s) in parts:
                row = sum(CHUNKS[k][1] for k, _ in parts[: parts.index((c, s))])
                return u, slice(row, row + CHUNKS[c][1])

    def send_needed(c):
        across(c).wait_recv()
        for s in range(2):
            u, rows = place(c, s)
            kv[u][me, rows] = both[c][table[s]]
            for d in range(1, PLANE):
                out_kv[u][d, rows] = both[c][table[2 * d + s]]
            if UNITS[u][-1] == (c, s):
                for d in range(1, PLANE):
                    third(u, d).start()

    def weigh(s, keys):
        scores = lax.dot_general(q[s], keys, NT, preferred_element_type=F32)
        return jnp.exp(50.0 * jnp.tanh(scores * 0.00125))

    def lanes(weights):
        total = weights[:, :128]
        for i in range(1, weights.shape[1] // 128):
            total = total + weights[:, 128 * i : 128 * (i + 1)]
        return total

    def attend_suffix(s):
        length = suffix_len[assign[req * 2 + s]]
        row = lax.broadcasted_iota(jnp.int32, (512, 256), 0) % 256
        key = lax.broadcasted_iota(jnp.int32, (512, 256), 1)
        weights = weigh(s, suf[s, :, :256])
        weights = jnp.where((key <= row) & (key < length), weights, 0.0)
        acc[s] = jnp.dot(weights.astype(BF), suf[s, :, 256:], preferred_element_type=F32)
        tot[s] = lanes(weights)

    def attend(c, s):
        u, rows = place(c, s)
        if UNITS[u][0] == (c, s):
            for d in range(1, PLANE):
                third(u, d).wait_recv()

        both_parts = kv[u][:, rows].reshape(-1, 512)
        weights = weigh(s, both_parts[:, :256])
        acc[s] += jnp.dot(weights.astype(BF), both_parts[:, 256:], preferred_element_type=F32)
        tot[s] += lanes(weights)

    def to_partner(i):
        return pltpu.make_async_remote_copy(
            src_ref=wt.at[pl.ds(pl.multiple_of(896 * i + COLS * (1 - core), 64), COLS)],
            dst_ref=wtr.at[pl.ds(COLS * i, COLS)],
            send_sem=ws.at[i], recv_sem=wr.at[i],
            device_id=(req, partner), device_id_type=MESH,
        )

    def turn_weights(i):
        if i == 0:
            loads[2].wait()
        wt[896 * i : 896 * (i + 1), :] = w[:, 896 * i : 896 * (i + 1)].T
        to_partner(i).start()

    def share(s):
        return pltpu.make_async_remote_copy(
            src_ref=att.at[s], dst_ref=attr.at[s], send_sem=ats.at[s], recv_sem=atr.at[s],
            device_id=(req, partner), device_id_type=MESH,
        )

    near, far, cross = z + 1 - 2 * (z % 2), (z + 2) % 4, 3 - z
    middle = ((z + 1) // 2) % 2
    ahead = near + middle * (cross - near)

    def to_near(s):
        return pltpu.make_async_remote_copy(
            src_ref=part.at[s, 1], dst_ref=landed.at[s, 1],
            send_sem=rs.at[s, 1], recv_sem=rr.at[s, 1],
            device_id=(req, 2 * near + core), device_id_type=MESH,
        )

    def to_far(s):
        return pltpu.make_async_remote_copy(
            src_ref=part.at[s, 2], dst_ref=landed.at[s, 2],
            send_sem=rs.at[s, 2], recv_sem=rr.at[s, 2],
            device_id=(req, 2 * far + core), device_id_type=MESH,
        )

    def to_ahead(s):
        return pltpu.make_async_remote_copy(
            src_ref=part.at[s, 0], dst_ref=landed.at[s, 3 * middle],
            send_sem=rs.at[s, 0], recv_sem=rr.at[s, 3 * middle],
            device_id=(req, 2 * ahead + core), device_id_type=MESH,
        )

    def arrived(s, i):
        return pltpu.make_async_remote_copy(
            src_ref=part.at[s, 0], dst_ref=landed.at[s, i],
            send_sem=rs.at[s, 0], recv_sem=rr.at[s, i],
            device_id=(req, 2 * near + core), device_id_type=MESH,
        )

    def project(s):
        total = jnp.sum(tot[s], axis=1, keepdims=True)
        value = (acc[s] / total).astype(BF)
        att[s, :, :256] = value[:256]
        att[s, :, 256:] = value[256:]
        share(s).start()

        def here(block):
            start = pl.multiple_of(896 * block + COLS * core, 64)
            return lax.dot_general(
                wt[pl.ds(start, COLS), :], att[s], NT, preferred_element_type=F32
            )

        def there(block):
            start = pl.multiple_of(COLS * block, 64)
            return lax.dot_general(
                wtr[pl.ds(start, COLS), :], attr[s], NT, preferred_element_type=F32
            )

        own[s] = here(cross)
        mid[s] = here(far)
        share(s).wait_recv()
        part[s, 0] = (own[s] + there(cross)).astype(BF)
        to_ahead(s).start()
        mid[s] += there(far)

        @pl.when(middle == 0)
        def _():
            part[s, 2] = mid[s].astype(BF)
            to_far(s).start()

        part[s, 1] = (here(near) + there(near)).astype(BF)
        to_near(s).start()
        own[s] = here(z) + there(z)

        @pl.when(middle == 1)
        def _():
            arrived(s, 0).wait_recv()
            part[s, 2] = (mid[s] + landed[s, 0].astype(F32)).astype(BF)
            to_far(s).start()

    def tell(s, d):
        return pltpu.make_async_remote_copy(
            src_ref=sq.at[s], dst_ref=sqr.at[s, d], send_sem=ss.at[s, d], recv_sem=sr.at[s, d],
            device_id=(req, (tp + d) % 8), device_id_type=MESH,
        )

    def gather_sums(s):
        @pl.when(middle == 1)
        def _():
            arrived(s, 3).wait_recv()
            own[s] += landed[s, 3].astype(F32)

        to_near(s).wait_recv()
        to_far(s).wait_recv()
        value = own[s] + landed[s, 1].astype(F32) + landed[s, 2].astype(F32)
        own[s] = value
        sq[s] = jnp.sum(value * value, axis=0, keepdims=True)

        @pl.loop(1, 8)
        def _(d):
            tell(s, d).start()

    def finish(s):
        @pl.loop(1, 8)
        def _(d):
            tell(s, d).wait_recv()

        squares = sq[s]
        for d in range(1, 8):
            squares = squares + sqr[s, d]
        scale = lax.rsqrt(squares / D + 1e-06)
        out[s] = (res[s].astype(F32) + own[s] * scale * gain[...]).astype(BF)

    def prepare():
        loads[0].wait()
        for s in range(2):
            for h in range(2):
                q[s, 256 * h : 256 * (h + 1)] = raw[s, :, h, :]
        loads[4].wait()
        gain[...] = jnp.broadcast_to(gain_row[...][None, :], (256, COLS)).T
        loads[1].wait()

    prepare()
    attend_suffix(0)
    send_across(0)
    attend_suffix(1)
    send_across(1)
    turn_weights(0)
    send_across(2)
    turn_weights(1)
    send_across(3)
    send_needed(0)
    turn_weights(2)
    turn_weights(3)
    send_needed(1)
    attend(0, 0)
    attend(0, 1)
    send_needed(2)
    attend(1, 0)
    attend(1, 1)
    send_needed(3)
    attend(2, 0)
    for i in range(4):
        to_partner(i).wait_recv()
    attend(3, 0)
    project(0)
    attend(2, 1)
    attend(3, 1)
    project(1)
    for c in range(len(CHUNKS)):
        across(c).wait_send()
    for k in range(len(CHUNKS)):
        for d in range(1, PLANE):
            first(k, d).wait_send()
    for u in range(len(UNITS)):
        for d in range(1, PLANE):
            third(u, d).wait_send()
    loads[3].wait()
    gather_sums(0)
    finish(0)
    gather_sums(1)
    finish(1)

    for i in range(4):
        to_partner(i).wait_send()
    for s in range(2):
        share(s).wait_send()
        to_near(s).wait_send()
        to_far(s).wait_send()
        to_ahead(s).wait_send()

        @pl.loop(1, 8)
        def _(d, s=s):
            tell(s, d).wait_send()


def local(
    queries, suffix_kv, prefix_kv, out_weight, residual, norm_gain, suffix_len, member, owner, assign
):
    suffix = suffix_kv.reshape(2, 256, 512)
    prefix = prefix_kv.reshape(PLANE, -1, 512)
    stream = jnp.transpose(residual, (0, 2, 1))
    anywhere = pl.BlockSpec(memory_space=pl.ANY)
    V = pltpu.VMEM
    DMA = pltpu.SemaphoreType.DMA

    def piece(rows):
        return V((PLANE, rows, 512), BF)

    pieces = [piece(rows) for _, rows in CHUNKS]
    units = [piece(sum(CHUNKS[c][1] for c, _ in parts)) for parts in UNITS]
    out = pl.pallas_call(
        kernel,
        name="prefill",
        out_shape=pltpu.VMEM((2, COLS, 256), BF),
        in_specs=[anywhere] * 10,
        out_specs=pl.BlockSpec(memory_space=pltpu.VMEM),
        scratch_shapes=[
            pieces, pieces, units, units,
            pltpu.SMEM((64,), jnp.int32), pltpu.SMEM((64,), jnp.int32), pltpu.SMEM((8,), jnp.int32),
            pltpu.SMEM((64,), jnp.int32), V((2, 256, 2, 256), BF), V((2, 512, 256), BF), V((2, 256, 512), BF), V((512, D), BF), V((D, 512), BF),
            V((D // 2, 512), BF), V((2, COLS, 256), BF), V((COLS,), F32), V((COLS, 256), F32),
            V((2, 512, 256), F32), V((2, 512, 128), F32), V((2, 256, 512), BF), V((2, 256, 512), BF),
            V((2, 3, COLS, 256), BF), V((2, COLS, 256), F32), V((2, COLS, 256), F32),
            V((2, 4, COLS, 256), BF), V((2, 1, 256), F32), V((2, 8, 1, 256), F32),
            pltpu.SMEM((2 * PLANE,), jnp.int32),
            DMA((9,)), DMA((LAST + 1,)), DMA((LAST + 1, PLANE)), DMA((LAST + 1, PLANE)),
            DMA((LAST + 1,)), DMA((LAST + 1,)), DMA((len(UNITS), PLANE)), DMA((len(UNITS), PLANE)),
            DMA((4,)), DMA((4,)), DMA((2,)), DMA((2,)), DMA((2, 3)), DMA((2, 4)),
            DMA((2, 8)), DMA((2, 8)),
        ],
        compiler_params=pltpu.CompilerParams(
            collective_id=0, has_side_effects=True, vmem_limit_bytes=56 * 2**20
        ),
    )(suffix_len, member, owner, assign, queries, suffix, prefix, out_weight, stream, norm_gain)
    return jnp.transpose(out, (0, 2, 1))


def solution(mesh):
    in_specs = (
        P("req", None, "tp", None),
        P("req", None, "tp", None),
        P("req", None, "tp", None),
        P("tp", None),
        P("req", None, "tp"),
        P("tp"),
        P(),
        P(),
        P(),
        P(),
    )
    out_specs = P("req", None, "tp")
    return jax.shard_map(local, mesh=mesh, in_specs=in_specs, out_specs=out_specs, check_vma=False)
```

```python
import jax
import jax.numpy as jnp
from jax import lax
from jax.experimental import pallas as pl
from jax.experimental.pallas import tpu as pltpu
from jax.sharding import PartitionSpec as P

D = 3584
MESH = pl.DeviceIdType.MESH
PLANE = 16
STEPS = [
    (0, 0), (2, 2), (2, 1), (1, 2), (2, 3), (3, 2), (1, 1), (3, 3),
    (1, 3), (3, 1), (2, 0), (0, 2), (1, 0), (0, 1), (3, 0), (0, 3),
]
CHUNKS = [(0, 16), (16, 16), (32, 16), (48, 16)]
LAST = len(CHUNKS) - 1
UNITS = [[(0, 0), (0, 1)], [(1, 0), (1, 1)], [(2, 0)], [(3, 0)], [(2, 1), (3, 1)]]
BF = jnp.bfloat16
F32 = jnp.float32
NT = (((1,), (1,)), ((), ()))
COLS = 448


def kernel(
    lens_hbm, member_hbm, owner_hbm, assign_hbm,
    q_hbm, suf_hbm, pre_hbm, w_hbm, res_hbm, gain_hbm,
    out,
    got, both, out_kv, kv,
    suffix_len, member, owner, assign, raw, q, suf, w, wt, wtr, res, gain_row, gain, acc, tot, att, attr,
    part, mid, own, landed, sq, sqr, table,
    local_sem, own_sem, p1s, p1r, zs, zr, p2s, p2r, ws, wr, ats, atr, rs, rr, ss, sr,
):
    req = lax.axis_index("req")
    tp = lax.axis_index("tp")
    half = req // PLANE
    me = req % PLANE
    mx, my = me % 4, me // 4
    z, core = tp // 2, tp % 2
    other_half = 1 - half
    partner = tp + 1 - 2 * core
    base = half * PLANE

    peers = [
        (my + dy + core * (dx - dy) + 4) % 4 * 4 + (mx + dx + core * (dy - dx) + 4) % 4
        for dx, dy in STEPS
    ]

    def local(i, src, dst):
        return pltpu.make_async_copy(src, dst, local_sem.at[i])

    loads = [
        local(0, q_hbm, raw), local(1, suf_hbm, suf), local(2, w_hbm, w),
        local(3, res_hbm, res), local(4, gain_hbm, gain_row),
        local(5, lens_hbm, suffix_len), local(6, member_hbm, member), local(7, owner_hbm, owner),
        local(8, assign_hbm, assign),
    ]

    barrier = pltpu.get_barrier_semaphore()

    pl.semaphore_signal(
        barrier, inc=1, device_id=(other_half * PLANE + me, tp), device_id_type=MESH
    )
    for d in range(1, PLANE):
        pl.semaphore_signal(barrier, inc=1, device_id=(base + peers[d], tp), device_id_type=MESH)
    for d in range(1, 8):
        pl.semaphore_signal(barrier, inc=1, device_id=(req, (tp + d) % 8), device_id_type=MESH)
    for load in loads:
        load.start()
    def span(c):
        return pl.ds(*CHUNKS[c])

    mine = [
        pltpu.make_async_copy(pre_hbm.at[me, span(k)], got[k].at[me], own_sem.at[k])
        for k in range(len(CHUNKS))
    ]
    for copy in mine:
        copy.start()
    pl.semaphore_wait(barrier, 23)

    def first(k, d):
        return pltpu.make_async_remote_copy(
            src_ref=pre_hbm.at[peers[d], span(k)], dst_ref=got[k].at[me],
            send_sem=p1s.at[k, d], recv_sem=p1r.at[k, d],
            device_id=(base + peers[d], tp), device_id_type=MESH,
        )

    for k in range(len(CHUNKS)):
        for d in range(1, PLANE):
            first(k, d).start()

    for load in loads[5:]:
        load.wait()

    for d in range(PLANE):
        for s in range(2):
            group = member[assign[(base + peers[d]) * 2 + s]] // 8
            apart = owner[group] // PLANE - half
            table[2 * d + s] = group + 8 * apart * apart

    def across(c):
        return pltpu.make_async_remote_copy(
            src_ref=both[c].at[pl.ds(0, 8)], dst_ref=both[c].at[pl.ds(8, 8)],
            send_sem=zs.at[c], recv_sem=zr.at[c],
            device_id=(other_half * PLANE + me, tp), device_id_type=MESH,
        )

    def send_across(c):
        mine[c].wait()
        for d in range(1, PLANE):
            first(c, d).wait_recv()
        for g in range(8):
            both[c][g] = got[c][owner[g] % PLANE]
        across(c).start()

    def third(u, d):
        return pltpu.make_async_remote_copy(
            src_ref=out_kv[u].at[d], dst_ref=kv[u].at[me],
            send_sem=p2s.at[u, d], recv_sem=p2r.at[u, d],
            device_id=(base + peers[d], tp), device_id_type=MESH,
        )

    def place(c, s):
        for u, parts in enumerate(UNITS):
            if (c, s) in parts:
                row = sum(CHUNKS[k][1] for k, _ in parts[: parts.index((c, s))])
                return u, slice(row, row + CHUNKS[c][1])

    def send_needed(c):
        across(c).wait_recv()
        for s in range(2):
            u, rows = place(c, s)
            kv[u][me, rows] = both[c][table[s]]
            for d in range(1, PLANE):
                out_kv[u][d, rows] = both[c][table[2 * d + s]]
            if UNITS[u][-1] == (c, s):
                for d in range(1, PLANE):
                    third(u, d).start()

    def weigh(s, keys):
        scores = lax.dot_general(q[s], keys, NT, preferred_element_type=F32)
        return jnp.exp(50.0 * jnp.tanh(scores * 0.00125))

    def lanes(weights):
        total = weights[:, :128]
        for i in range(1, weights.shape[1] // 128):
            total = total + weights[:, 128 * i : 128 * (i + 1)]
        return total

    def attend_suffix(s):
        length = suffix_len[assign[req * 2 + s]]
        row = lax.broadcasted_iota(jnp.int32, (512, 256), 0) % 256
        key = lax.broadcasted_iota(jnp.int32, (512, 256), 1)
        weights = weigh(s, suf[s, :, :256])
        weights = jnp.where((key <= row) & (key < length), weights, 0.0)
        acc[s] = jnp.dot(weights.astype(BF), suf[s, :, 256:], preferred_element_type=F32)
        tot[s] = lanes(weights)

    def attend(c, s):
        u, rows = place(c, s)
        if UNITS[u][0] == (c, s):
            for d in range(1, PLANE):
                third(u, d).wait_recv()

        both_parts = kv[u][:, rows].reshape(-1, 512)
        weights = weigh(s, both_parts[:, :256])
        acc[s] += jnp.dot(weights.astype(BF), both_parts[:, 256:], preferred_element_type=F32)
        tot[s] += lanes(weights)

    def to_partner(i):
        return pltpu.make_async_remote_copy(
            src_ref=wt.at[pl.ds(pl.multiple_of(896 * i + COLS * (1 - core), 64), COLS)],
            dst_ref=wtr.at[pl.ds(COLS * i, COLS)],
            send_sem=ws.at[i], recv_sem=wr.at[i],
            device_id=(req, partner), device_id_type=MESH,
        )

    def turn_weights(i):
        if i == 0:
            loads[2].wait()
        wt[896 * i : 896 * (i + 1), :] = w[:, 896 * i : 896 * (i + 1)].T
        to_partner(i).start()

    def share(s):
        return pltpu.make_async_remote_copy(
            src_ref=att.at[s], dst_ref=attr.at[s], send_sem=ats.at[s], recv_sem=atr.at[s],
            device_id=(req, partner), device_id_type=MESH,
        )

    near, far, cross = z + 1 - 2 * (z % 2), (z + 2) % 4, 3 - z
    middle = ((z + 1) // 2) % 2
    ahead = near + middle * (cross - near)

    def to_near(s):
        return pltpu.make_async_remote_copy(
            src_ref=part.at[s, 1], dst_ref=landed.at[s, 1],
            send_sem=rs.at[s, 1], recv_sem=rr.at[s, 1],
            device_id=(req, 2 * near + core), device_id_type=MESH,
        )

    def to_far(s):
        return pltpu.make_async_remote_copy(
            src_ref=part.at[s, 2], dst_ref=landed.at[s, 2],
            send_sem=rs.at[s, 2], recv_sem=rr.at[s, 2],
            device_id=(req, 2 * far + core), device_id_type=MESH,
        )

    def to_ahead(s):
        return pltpu.make_async_remote_copy(
            src_ref=part.at[s, 0], dst_ref=landed.at[s, 3 * middle],
            send_sem=rs.at[s, 0], recv_sem=rr.at[s, 3 * middle],
            device_id=(req, 2 * ahead + core), device_id_type=MESH,
        )

    def arrived(s, i):
        return pltpu.make_async_remote_copy(
            src_ref=part.at[s, 0], dst_ref=landed.at[s, i],
            send_sem=rs.at[s, 0], recv_sem=rr.at[s, i],
            device_id=(req, 2 * near + core), device_id_type=MESH,
        )

    def project(s):
        total = jnp.sum(tot[s], axis=1, keepdims=True)
        value = (acc[s] / total).astype(BF)
        att[s, :, :256] = value[:256]
        att[s, :, 256:] = value[256:]
        share(s).start()

        def here(block):
            start = pl.multiple_of(896 * block + COLS * core, 64)
            return lax.dot_general(
                wt[pl.ds(start, COLS), :], att[s], NT, preferred_element_type=F32
            )

        def there(block):
            start = pl.multiple_of(COLS * block, 64)
            return lax.dot_general(
                wtr[pl.ds(start, COLS), :], attr[s], NT, preferred_element_type=F32
            )

        own[s] = here(cross)
        mid[s] = here(far)
        share(s).wait_recv()
        part[s, 0] = (own[s] + there(cross)).astype(BF)
        to_ahead(s).start()
        mid[s] += there(far)

        @pl.when(middle == 0)
        def _():
            part[s, 2] = mid[s].astype(BF)
            to_far(s).start()

        part[s, 1] = (here(near) + there(near)).astype(BF)
        to_near(s).start()
        own[s] = here(z) + there(z)

        @pl.when(middle == 1)
        def _():
            arrived(s, 0).wait_recv()
            part[s, 2] = (mid[s] + landed[s, 0].astype(F32)).astype(BF)
            to_far(s).start()

    def tell(s, d):
        return pltpu.make_async_remote_copy(
            src_ref=sq.at[s], dst_ref=sqr.at[s, d], send_sem=ss.at[s, d], recv_sem=sr.at[s, d],
            device_id=(req, (tp + d) % 8), device_id_type=MESH,
        )

    def gather_sums(s):
        @pl.when(middle == 1)
        def _():
            arrived(s, 3).wait_recv()
            own[s] += landed[s, 3].astype(F32)

        to_near(s).wait_recv()
        to_far(s).wait_recv()
        value = own[s] + landed[s, 1].astype(F32) + landed[s, 2].astype(F32)
        own[s] = value
        sq[s] = jnp.sum(value * value, axis=0, keepdims=True)

        @pl.loop(1, 8)
        def _(d):
            tell(s, d).start()

    def finish(s):
        @pl.loop(1, 8)
        def _(d):
            tell(s, d).wait_recv()

        squares = sq[s]
        for d in range(1, 8):
            squares = squares + sqr[s, d]
        scale = lax.rsqrt(squares / D + 1e-06)
        out[s] = (res[s].astype(F32) + own[s] * scale * gain[...]).astype(BF)

    def prepare():
        loads[0].wait()
        for s in range(2):
            for h in range(2):
                q[s, 256 * h : 256 * (h + 1)] = raw[s, :, h, :]
        loads[4].wait()
        gain[...] = jnp.broadcast_to(gain_row[...][None, :], (256, COLS)).T
        loads[1].wait()

    prepare()
    attend_suffix(0)
    send_across(0)
    attend_suffix(1)
    send_across(1)
    turn_weights(0)
    send_across(2)
    turn_weights(1)
    send_across(3)
    send_needed(0)
    turn_weights(2)
    turn_weights(3)
    send_needed(1)
    attend(0, 0)
    attend(0, 1)
    send_needed(2)
    attend(1, 0)
    attend(1, 1)
    send_needed(3)
    attend(2, 0)
    for i in range(4):
        to_partner(i).wait_recv()
    attend(3, 0)
    project(0)
    attend(2, 1)
    attend(3, 1)
    project(1)
    for c in range(len(CHUNKS)):
        across(c).wait_send()
    for k in range(len(CHUNKS)):
        for d in range(1, PLANE):
            first(k, d).wait_send()
    for u in range(len(UNITS)):
        for d in range(1, PLANE):
            third(u, d).wait_send()
    loads[3].wait()
    gather_sums(0)
    finish(0)
    gather_sums(1)
    finish(1)

    for i in range(4):
        to_partner(i).wait_send()
    for s in range(2):
        share(s).wait_send()
        to_near(s).wait_send()
        to_far(s).wait_send()
        to_ahead(s).wait_send()

        @pl.loop(1, 8)
        def _(d, s=s):
            tell(s, d).wait_send()


def local(
    queries, suffix_kv, prefix_kv, out_weight, residual, norm_gain, suffix_len, member, owner, assign
):
    suffix = suffix_kv.reshape(2, 256, 512)
    prefix = prefix_kv.reshape(PLANE, -1, 512)
    stream = jnp.transpose(residual, (0, 2, 1))
    anywhere = pl.BlockSpec(memory_space=pl.ANY)
    V = pltpu.VMEM
    DMA = pltpu.SemaphoreType.DMA

    def piece(rows):
        return V((PLANE, rows, 512), BF)

    pieces = [piece(rows) for _, rows in CHUNKS]
    units = [piece(sum(CHUNKS[c][1] for c, _ in parts)) for parts in UNITS]
    out = pl.pallas_call(
        kernel,
        name="prefill",
        out_shape=pltpu.VMEM((2, COLS, 256), BF),
        in_specs=[anywhere] * 10,
        out_specs=pl.BlockSpec(memory_space=pltpu.VMEM),
        scratch_shapes=[
            pieces, pieces, units, units,
            pltpu.SMEM((64,), jnp.int32), pltpu.SMEM((64,), jnp.int32), pltpu.SMEM((8,), jnp.int32),
            pltpu.SMEM((64,), jnp.int32), V((2, 256, 2, 256), BF), V((2, 512, 256), BF), V((2, 256, 512), BF), V((512, D), BF), V((D, 512), BF),
            V((D // 2, 512), BF), V((2, COLS, 256), BF), V((COLS,), F32), V((COLS, 256), F32),
            V((2, 512, 256), F32), V((2, 512, 128), F32), V((2, 256, 512), BF), V((2, 256, 512), BF),
            V((2, 3, COLS, 256), BF), V((2, COLS, 256), F32), V((2, COLS, 256), F32),
            V((2, 4, COLS, 256), BF), V((2, 1, 256), F32), V((2, 8, 1, 256), F32),
            pltpu.SMEM((2 * PLANE,), jnp.int32),
            DMA((9,)), DMA((LAST + 1,)), DMA((LAST + 1, PLANE)), DMA((LAST + 1, PLANE)),
            DMA((LAST + 1,)), DMA((LAST + 1,)), DMA((len(UNITS), PLANE)), DMA((len(UNITS), PLANE)),
            DMA((4,)), DMA((4,)), DMA((2,)), DMA((2,)), DMA((2, 3)), DMA((2, 4)),
            DMA((2, 8)), DMA((2, 8)),
        ],
        compiler_params=pltpu.CompilerParams(
            collective_id=0, has_side_effects=True, vmem_limit_bytes=56 * 2**20
        ),
    )(suffix_len, member, owner, assign, queries, suffix, prefix, out_weight, stream, norm_gain)
    return jnp.transpose(out, (0, 2, 1))


def solution(mesh):
    in_specs = (
        P("req", None, "tp", None),
        P("req", None, "tp", None),
        P("req", None, "tp", None),
        P("tp", None),
        P("req", None, "tp"),
        P("tp"),
        P(),
        P(),
        P(),
        P(),
    )
    out_specs = P("req", None, "tp")
    return jax.shard_map(local, mesh=mesh, in_specs=in_specs, out_specs=out_specs, check_vma=False)
```

```python
import jax
import jax.numpy as jnp
from jax import lax
from jax.experimental import pallas as pl
from jax.experimental.pallas import tpu as pltpu
from jax.sharding import PartitionSpec as P

D = 3584
MESH = pl.DeviceIdType.MESH
PLANE = 16
STEPS = [
    (0, 0), (2, 2), (2, 1), (1, 2), (2, 3), (3, 2), (1, 1), (3, 3),
    (1, 3), (3, 1), (2, 0), (0, 2), (1, 0), (0, 1), (3, 0), (0, 3),
]
CHUNKS = [(0, 16), (16, 16), (32, 16), (48, 16)]
LAST = len(CHUNKS) - 1
UNITS = [[(0, 0), (0, 1)], [(1, 0), (1, 1)], [(2, 0)], [(3, 0)], [(2, 1), (3, 1)]]
BF = jnp.bfloat16
F32 = jnp.float32
NT = (((1,), (1,)), ((), ()))
COLS = 448


def kernel(
    lens_hbm, member_hbm, owner_hbm, assign_hbm,
    q_hbm, suf_hbm, pre_hbm, w_hbm, res_hbm, gain_hbm,
    out,
    got, both, out_kv, kv,
    suffix_len, member, owner, assign, raw, q, suf, w, wt, wtr, res, gain_row, gain, acc, tot, att, attr,
    part, mid, own, landed, sq, sqr, table,
    local_sem, own_sem, p1s, p1r, zs, zr, p2s, p2r, ws, wr, ats, atr, rs, rr, ss, sr,
):
    req = lax.axis_index("req")
    tp = lax.axis_index("tp")
    half = req // PLANE
    me = req % PLANE
    mx, my = me % 4, me // 4
    z, core = tp // 2, tp % 2
    other_half = 1 - half
    partner = tp + 1 - 2 * core
    base = half * PLANE

    peers = [
        (my + dy + core * (dx - dy) + 4) % 4 * 4 + (mx + dx + core * (dy - dx) + 4) % 4
        for dx, dy in STEPS
    ]

    def local(i, src, dst):
        return pltpu.make_async_copy(src, dst, local_sem.at[i])

    loads = [
        local(0, q_hbm, raw), local(1, suf_hbm, suf), local(2, w_hbm, w),
        local(3, res_hbm, res), local(4, gain_hbm, gain_row),
        local(5, lens_hbm, suffix_len), local(6, member_hbm, member), local(7, owner_hbm, owner),
        local(8, assign_hbm, assign),
    ]

    barrier = pltpu.get_barrier_semaphore()

    pl.semaphore_signal(
        barrier, inc=1, device_id=(other_half * PLANE + me, tp), device_id_type=MESH
    )
    for d in range(1, PLANE):
        pl.semaphore_signal(barrier, inc=1, device_id=(base + peers[d], tp), device_id_type=MESH)
    for d in range(1, 8):
        pl.semaphore_signal(barrier, inc=1, device_id=(req, (tp + d) % 8), device_id_type=MESH)
    for load in loads:
        load.start()
    def span(c):
        return pl.ds(*CHUNKS[c])

    mine = [
        pltpu.make_async_copy(pre_hbm.at[me, span(k)], got[k].at[me], own_sem.at[k])
        for k in range(len(CHUNKS))
    ]
    for copy in mine:
        copy.start()
    pl.semaphore_wait(barrier, 23)

    def first(k, d):
        return pltpu.make_async_remote_copy(
            src_ref=pre_hbm.at[peers[d], span(k)], dst_ref=got[k].at[me],
            send_sem=p1s.at[k, d], recv_sem=p1r.at[k, d],
            device_id=(base + peers[d], tp), device_id_type=MESH,
        )

    for k in range(len(CHUNKS)):
        for d in range(1, PLANE):
            first(k, d).start()

    for load in loads[5:]:
        load.wait()

    for d in range(PLANE):
        for s in range(2):
            group = member[assign[(base + peers[d]) * 2 + s]] // 8
            apart = owner[group] // PLANE - half
            table[2 * d + s] = group + 8 * apart * apart

    def across(c):
        return pltpu.make_async_remote_copy(
            src_ref=both[c].at[pl.ds(0, 8)], dst_ref=both[c].at[pl.ds(8, 8)],
            send_sem=zs.at[c], recv_sem=zr.at[c],
            device_id=(other_half * PLANE + me, tp), device_id_type=MESH,
        )

    def send_across(c):
        mine[c].wait()
        for d in range(1, PLANE):
            first(c, d).wait_recv()
        for g in range(8):
            both[c][g] = got[c][owner[g] % PLANE]
        across(c).start()

    def third(u, d):
        return pltpu.make_async_remote_copy(
            src_ref=out_kv[u].at[d], dst_ref=kv[u].at[me],
            send_sem=p2s.at[u, d], recv_sem=p2r.at[u, d],
            device_id=(base + peers[d], tp), device_id_type=MESH,
        )

    def place(c, s):
        for u, parts in enumerate(UNITS):
            if (c, s) in parts:
                row = sum(CHUNKS[k][1] for k, _ in parts[: parts.index((c, s))])
                return u, slice(row, row + CHUNKS[c][1])

    def send_needed(c):
        across(c).wait_recv()
        for s in range(2):
            u, rows = place(c, s)
            kv[u][me, rows] = both[c][table[s]]
            for d in range(1, PLANE):
                out_kv[u][d, rows] = both[c][table[2 * d + s]]
            if UNITS[u][-1] == (c, s):
                for d in range(1, PLANE):
                    third(u, d).start()

    def weigh(s, keys):
        scores = lax.dot_general(q[s], keys, NT, preferred_element_type=F32)
        return jnp.exp(50.0 * jnp.tanh(scores * 0.00125))

    def lanes(weights):
        total = weights[:, :128]
        for i in range(1, weights.shape[1] // 128):
            total = total + weights[:, 128 * i : 128 * (i + 1)]
        return total

    def attend_suffix(s):
        length = suffix_len[assign[req * 2 + s]]
        row = lax.broadcasted_iota(jnp.int32, (512, 256), 0) % 256
        key = lax.broadcasted_iota(jnp.int32, (512, 256), 1)
        weights = weigh(s, suf[s, :, :256])
        weights = jnp.where((key <= row) & (key < length), weights, 0.0)
        acc[s] = jnp.dot(weights.astype(BF), suf[s, :, 256:], preferred_element_type=F32)
        tot[s] = lanes(weights)

    def attend(c, s):
        u, rows = place(c, s)
        if UNITS[u][0] == (c, s):
            for d in range(1, PLANE):
                third(u, d).wait_recv()

        both_parts = kv[u][:, rows].reshape(-1, 512)
        weights = weigh(s, both_parts[:, :256])
        acc[s] += jnp.dot(weights.astype(BF), both_parts[:, 256:], preferred_element_type=F32)
        tot[s] += lanes(weights)

    def to_partner(i):
        return pltpu.make_async_remote_copy(
            src_ref=wt.at[pl.ds(pl.multiple_of(896 * i + COLS * (1 - core), 64), COLS)],
            dst_ref=wtr.at[pl.ds(COLS * i, COLS)],
            send_sem=ws.at[i], recv_sem=wr.at[i],
            device_id=(req, partner), device_id_type=MESH,
        )

    def turn_weights(i):
        if i == 0:
            loads[2].wait()
        wt[896 * i : 896 * (i + 1), :] = w[:, 896 * i : 896 * (i + 1)].T
        to_partner(i).start()

    def share(s):
        return pltpu.make_async_remote_copy(
            src_ref=att.at[s], dst_ref=attr.at[s], send_sem=ats.at[s], recv_sem=atr.at[s],
            device_id=(req, partner), device_id_type=MESH,
        )

    near, far, cross = z + 1 - 2 * (z % 2), (z + 2) % 4, 3 - z
    middle = ((z + 1) // 2) % 2
    ahead = near + middle * (cross - near)

    def to_near(s):
        return pltpu.make_async_remote_copy(
            src_ref=part.at[s, 1], dst_ref=landed.at[s, 1],
            send_sem=rs.at[s, 1], recv_sem=rr.at[s, 1],
            device_id=(req, 2 * near + core), device_id_type=MESH,
        )

    def to_far(s):
        return pltpu.make_async_remote_copy(
            src_ref=part.at[s, 2], dst_ref=landed.at[s, 2],
            send_sem=rs.at[s, 2], recv_sem=rr.at[s, 2],
            device_id=(req, 2 * far + core), device_id_type=MESH,
        )

    def to_ahead(s):
        return pltpu.make_async_remote_copy(
            src_ref=part.at[s, 0], dst_ref=landed.at[s, 3 * middle],
            send_sem=rs.at[s, 0], recv_sem=rr.at[s, 3 * middle],
            device_id=(req, 2 * ahead + core), device_id_type=MESH,
        )

    def arrived(s, i):
        return pltpu.make_async_remote_copy(
            src_ref=part.at[s, 0], dst_ref=landed.at[s, i],
            send_sem=rs.at[s, 0], recv_sem=rr.at[s, i],
            device_id=(req, 2 * near + core), device_id_type=MESH,
        )

    def project(s):
        total = jnp.sum(tot[s], axis=1, keepdims=True)
        value = (acc[s] / total).astype(BF)
        att[s, :, :256] = value[:256]
        att[s, :, 256:] = value[256:]
        share(s).start()

        def here(block):
            start = pl.multiple_of(896 * block + COLS * core, 64)
            return lax.dot_general(
                wt[pl.ds(start, COLS), :], att[s], NT, preferred_element_type=F32
            )

        def there(block):
            start = pl.multiple_of(COLS * block, 64)
            return lax.dot_general(
                wtr[pl.ds(start, COLS), :], attr[s], NT, preferred_element_type=F32
            )

        own[s] = here(cross)
        mid[s] = here(far)
        share(s).wait_recv()
        part[s, 0] = (own[s] + there(cross)).astype(BF)
        to_ahead(s).start()
        mid[s] += there(far)

        @pl.when(middle == 0)
        def _():
            part[s, 2] = mid[s].astype(BF)
            to_far(s).start()

        part[s, 1] = (here(near) + there(near)).astype(BF)
        to_near(s).start()
        own[s] = here(z) + there(z)

        @pl.when(middle == 1)
        def _():
            arrived(s, 0).wait_recv()
            part[s, 2] = (mid[s] + landed[s, 0].astype(F32)).astype(BF)
            to_far(s).start()

    def tell(s, d):
        return pltpu.make_async_remote_copy(
            src_ref=sq.at[s], dst_ref=sqr.at[s, d], send_sem=ss.at[s, d], recv_sem=sr.at[s, d],
            device_id=(req, (tp + d) % 8), device_id_type=MESH,
        )

    def gather_sums(s):
        @pl.when(middle == 1)
        def _():
            arrived(s, 3).wait_recv()
            own[s] += landed[s, 3].astype(F32)

        to_near(s).wait_recv()
        own[s] += landed[s, 1].astype(F32)
        to_far(s).wait_recv()
        value = own[s] + landed[s, 2].astype(F32)
        own[s] = value
        sq[s] = jnp.sum(value * value, axis=0, keepdims=True)

        @pl.loop(1, 8)
        def _(d):
            tell(s, d).start()

    def finish(s):
        @pl.loop(1, 8)
        def _(d):
            tell(s, d).wait_recv()

        squares = sq[s]
        for d in range(1, 8):
            squares = squares + sqr[s, d]
        scale = lax.rsqrt(squares / D + 1e-06)
        out[s] = (res[s].astype(F32) + own[s] * scale * gain[...]).astype(BF)

    def prepare():
        loads[0].wait()
        for s in range(2):
            for h in range(2):
                q[s, 256 * h : 256 * (h + 1)] = raw[s, :, h, :]
        loads[4].wait()
        gain[...] = jnp.broadcast_to(gain_row[...][None, :], (256, COLS)).T
        loads[1].wait()

    prepare()
    attend_suffix(0)
    send_across(0)
    attend_suffix(1)
    send_across(1)
    turn_weights(0)
    send_across(2)
    turn_weights(1)
    send_across(3)
    send_needed(0)
    turn_weights(2)
    turn_weights(3)
    send_needed(1)
    attend(0, 0)
    attend(0, 1)
    send_needed(2)
    attend(1, 0)
    attend(1, 1)
    send_needed(3)
    attend(2, 0)
    for i in range(4):
        to_partner(i).wait_recv()
    attend(3, 0)
    project(0)
    attend(2, 1)
    attend(3, 1)
    project(1)
    for c in range(len(CHUNKS)):
        across(c).wait_send()
    for k in range(len(CHUNKS)):
        for d in range(1, PLANE):
            first(k, d).wait_send()
    for u in range(len(UNITS)):
        for d in range(1, PLANE):
            third(u, d).wait_send()
    loads[3].wait()
    gather_sums(0)
    finish(0)
    gather_sums(1)
    finish(1)

    for i in range(4):
        to_partner(i).wait_send()
    for s in range(2):
        share(s).wait_send()
        to_near(s).wait_send()
        to_far(s).wait_send()
        to_ahead(s).wait_send()

        @pl.loop(1, 8)
        def _(d, s=s):
            tell(s, d).wait_send()


def local(
    queries, suffix_kv, prefix_kv, out_weight, residual, norm_gain, suffix_len, member, owner, assign
):
    suffix = suffix_kv.reshape(2, 256, 512)
    prefix = prefix_kv.reshape(PLANE, -1, 512)
    stream = jnp.transpose(residual, (0, 2, 1))
    anywhere = pl.BlockSpec(memory_space=pl.ANY)
    V = pltpu.VMEM
    DMA = pltpu.SemaphoreType.DMA

    def piece(rows):
        return V((PLANE, rows, 512), BF)

    pieces = [piece(rows) for _, rows in CHUNKS]
    units = [piece(sum(CHUNKS[c][1] for c, _ in parts)) for parts in UNITS]
    out = pl.pallas_call(
        kernel,
        name="prefill",
        out_shape=pltpu.VMEM((2, COLS, 256), BF),
        in_specs=[anywhere] * 10,
        out_specs=pl.BlockSpec(memory_space=pltpu.VMEM),
        scratch_shapes=[
            pieces, pieces, units, units,
            pltpu.SMEM((64,), jnp.int32), pltpu.SMEM((64,), jnp.int32), pltpu.SMEM((8,), jnp.int32),
            pltpu.SMEM((64,), jnp.int32), V((2, 256, 2, 256), BF), V((2, 512, 256), BF), V((2, 256, 512), BF), V((512, D), BF), V((D, 512), BF),
            V((D // 2, 512), BF), V((2, COLS, 256), BF), V((COLS,), F32), V((COLS, 256), F32),
            V((2, 512, 256), F32), V((2, 512, 128), F32), V((2, 256, 512), BF), V((2, 256, 512), BF),
            V((2, 3, COLS, 256), BF), V((2, COLS, 256), F32), V((2, COLS, 256), F32),
            V((2, 4, COLS, 256), BF), V((2, 1, 256), F32), V((2, 8, 1, 256), F32),
            pltpu.SMEM((2 * PLANE,), jnp.int32),
            DMA((9,)), DMA((LAST + 1,)), DMA((LAST + 1, PLANE)), DMA((LAST + 1, PLANE)),
            DMA((LAST + 1,)), DMA((LAST + 1,)), DMA((len(UNITS), PLANE)), DMA((len(UNITS), PLANE)),
            DMA((4,)), DMA((4,)), DMA((2,)), DMA((2,)), DMA((2, 3)), DMA((2, 4)),
            DMA((2, 8)), DMA((2, 8)),
        ],
        compiler_params=pltpu.CompilerParams(
            collective_id=0, has_side_effects=True, vmem_limit_bytes=56 * 2**20
        ),
    )(suffix_len, member, owner, assign, queries, suffix, prefix, out_weight, stream, norm_gain)
    return jnp.transpose(out, (0, 2, 1))


def solution(mesh):
    in_specs = (
        P("req", None, "tp", None),
        P("req", None, "tp", None),
        P("req", None, "tp", None),
        P("tp", None),
        P("req", None, "tp"),
        P("tp"),
        P(),
        P(),
        P(),
        P(),
    )
    out_specs = P("req", None, "tp")
    return jax.shard_map(local, mesh=mesh, in_specs=in_specs, out_specs=out_specs, check_vma=False)
```
